256 devices in a mesh: dp: 16 (over y, x_hi, core), mp: 16 (over z, x_lo).
Axes of the slice: x: 4 (x_hi: 2, x_lo: 2; x = x_hi * 2 + x_lo), y: 4, z: 8, core: 2. Of those that a mesh axis runs over, the one named last changes fastest.
Arguments:
- tokens: bfloat16 [16384, 2048], P(('dp', 'mp')), may hold values from -6 to 6
- norm_gain: float32 [2048], replicated, may hold values from 0.1 to 1.9
- mlp_gain: float32 [2048], replicated, may hold values from 0.1 to 1.9
- lengths: int32 [16], P('dp'), may hold values from 1 to 1024, as said below
- log_decay: float32 [16384, 8], P('dp'), as said below
- query_master: float32 [2048, 2048], P(('dp', 'mp')), may hold values from -0.125 to 0.125
- key_master: float32 [2048, 2048], P(('dp', 'mp')), may hold values from -0.125 to 0.125
- value_master: float32 [2048, 4096], P(('dp', 'mp')), may hold values from -0.125 to 0.125
- swish_master: float32 [2048, 4096], P(('dp', 'mp')), may hold values from -0.125 to 0.125
- output_master: float32 [4096, 2048], P(None, ('dp', 'mp')), may hold values from -0.09375 to 0.09375
- ffn_gate_master: float32 [2048, 4096], P(('dp', 'mp')), may hold values from -0.125 to 0.125
- ffn_up_master: float32 [2048, 4096], P(('dp', 'mp')), may hold values from -0.125 to 0.125
Outputs:
- residual: bfloat16 [16384, 2048], P(('dp', 'mp'))
- hidden: bfloat16 [16384, 4096], P('dp', 'mp')
The draws below stay inside these ranges and needn't reach their ends.
Inputs may be any that keep to these rules, and one draw needn't show every extreme that they name: `lengths`: given length of each prompt; in every draw some prompt has exactly 1024 tokens and some has 1. `log_decay`: Negative.
All inputs are finite; a program needn't handle non-finite values.
Results may differ from the reference program's by a relative error of at most 0.023.
Values may be sent and summed in bfloat16 or wider, within the bound.
A program may use at most 128 MiB of HBM per device.

```python
import math
import jax
import jax.numpy as jnp
from jax import lax

D = 2048
H = 8
DK = 256
DV = 512
FF = 4096
REQUEST_SPAN = 1024
KEYS = 2048
VALS = 4096
REQUEST_TOTAL = 16
TOKENS = 16384


def draw_lengths(key, part):
    first_key, second_key = jax.random.split(key)
    drawn_numbers = jax.random.randint(first_key, (REQUEST_TOTAL,), 1, REQUEST_SPAN + 1)
    chosen = jax.random.permutation(second_key, REQUEST_TOTAL)
    drawn_numbers = drawn_numbers.at[chosen[0]].set(REQUEST_SPAN)
    drawn_numbers = drawn_numbers.at[chosen[1]].set(1)
    return drawn_numbers.astype(jnp.int32)


def draw_log_decay(key, part):
    fading_seed_handle, coarse_seed_handle, spike_seed_handle, fill_seed_handle = jax.random.split(key, 4)
    lowest, highest = (math.log(0.2 / REQUEST_SPAN), math.log(30.0 / REQUEST_SPAN))
    depth_low = 0.5
    fading_factors = jnp.exp(jax.random.uniform(fading_seed_handle, (REQUEST_TOTAL, 1, H), jnp.float32, lowest, highest))
    coarse_spans = jax.random.uniform(coarse_seed_handle, (REQUEST_TOTAL, REQUEST_SPAN, H), jnp.float32, 0.5, 1.5)
    spike_spans = jax.random.randint(spike_seed_handle, (REQUEST_TOTAL, REQUEST_SPAN, 1), 0, REQUEST_SPAN) < 3
    request_fill_level = jnp.log(jax.random.uniform(fill_seed_handle, (REQUEST_TOTAL, REQUEST_SPAN, H), jnp.float32, depth_low, 0.8))
    drawn_numbers = -fading_factors * coarse_spans + jnp.where(spike_spans, request_fill_level, 0.0)
    return drawn_numbers.reshape(REQUEST_TOTAL * REQUEST_SPAN, H).astype(jnp.float32)


def shard_levels(key, shape, cuts, low, top_value):
    loudness, own = 1.0, jax.random.fold_in(key, 6)
    for dim, parts in cuts:
        draws = jnp.exp(jax.random.uniform(jax.random.fold_in(own, dim), (parts,), jnp.float32, low / len(cuts), top_value / len(cuts)))
        loudness = loudness * jnp.repeat(draws, shape[dim] // parts).reshape([-1 if axis == dim else 1 for axis in range(len(shape))])
    return loudness


def scatter_about(rng, shape, deviation, limit, cuts=(), held_as=jnp.bfloat16):
    loudness = shard_levels(rng, shape, cuts, -0.22, 0.18) if cuts else 1.0
    values = jax.random.normal(rng, shape, jnp.float32) * deviation * loudness
    return jnp.minimum(jnp.maximum(values, -limit), limit).astype(held_as)


def setup_inputs(seed: int = 0) -> dict:
    splits = jax.random.split(jax.random.key(seed), 13)
    return {
        "tokens": scatter_about(splits[0], (TOKENS, D), 1.0, 6.0, ((0, 256),)),
        "norm_gain": jnp.clip(1.0 + 0.18 * jax.random.normal(splits[1], (D,), jnp.float32), 0.1, 1.9),
        "mlp_gain": jnp.clip(1.0 + 0.18 * jax.random.normal(splits[2], (D,), jnp.float32), 0.1, 1.9),
        "lengths": draw_lengths(jax.random.fold_in(splits[12], 71), 0),
        "log_decay": draw_log_decay(jax.random.fold_in(splits[12], 71), 0),
        "query_master": scatter_about(splits[5], (D, KEYS), D ** -0.5, 0.125, ((0, 256),), jnp.float32),
        "key_master": scatter_about(splits[6], (D, KEYS), D ** -0.5, 0.125, ((0, 256),), jnp.float32),
        "value_master": scatter_about(splits[7], (D, VALS), D ** -0.5, 0.125, ((0, 256),), jnp.float32),
        "swish_master": scatter_about(splits[8], (D, VALS), D ** -0.5, 0.125, ((0, 256),), jnp.float32),
        "output_master": scatter_about(splits[9], (VALS, D), VALS ** -0.5, 0.09375, ((1, 256),), jnp.float32),
        "ffn_gate_master": scatter_about(splits[10], (D, FF), D ** -0.5, 0.125, ((0, 256),), jnp.float32),
        "ffn_up_master": scatter_about(splits[11], (D, FF), D ** -0.5, 0.125, ((0, 256),), jnp.float32),
    }


def rms_rows(row_block, gain_vec):
    values = row_block.astype(jnp.float32)
    scale = lax.rsqrt(lax.optimization_barrier(jnp.mean(values * values, axis=-1, keepdims=True)) + 1e-06)
    return (values * scale * gain_vec.astype(jnp.float32)).astype(jnp.bfloat16)

def rotate(values, places, first_channel):
    columns = values.shape[1]
    channel = (first_channel + jnp.arange(columns, dtype=jnp.int32)) % DK
    paired = (channel // 2 * 2).astype(jnp.float32)
    frequency = jnp.exp(paired * (-math.log(10000.0) / DK))
    angles = places.astype(jnp.float32)[:, None] * frequency[None, :]
    couples = values.reshape(values.shape[0], columns // 2, 2)
    turned = jnp.stack([-couples[:, :, 1], couples[:, :, 0]], axis=-1).reshape(values.shape)
    return values * jnp.cos(angles) + turned * jnp.sin(angles)

def retain_prompt(prompt_items):
    q_prompt, k_prompt, v_prompt, running = prompt_items
    scores = jnp.einsum('thd,shd->hts', q_prompt.astype(jnp.float32), k_prompt.astype(jnp.float32)) * DK ** (-0.5)
    decay_gap = running.T[:, :, None] - running.T[:, None, :]
    causal_mask = jnp.arange(REQUEST_SPAN, dtype=jnp.int32)[:, None] >= jnp.arange(REQUEST_SPAN, dtype=jnp.int32)[None, :]
    weights = (scores * jnp.exp(jnp.where(causal_mask[None], decay_gap, -jnp.inf))).astype(jnp.bfloat16)
    return jnp.einsum('hts,shd->thd', weights.astype(jnp.float32), v_prompt.astype(jnp.float32))

def reference(tokens, norm_gain, mlp_gain, lengths, log_decay, query_master, key_master, value_master, swish_master, output_master, ffn_gate_master, ffn_up_master):
    normed_in = rms_rows(tokens, norm_gain)
    places = jnp.arange(TOKENS, dtype=jnp.int32) % REQUEST_SPAN
    queries = rotate(jnp.dot(normed_in, query_master.astype(jnp.bfloat16), preferred_element_type=jnp.float32), places, 0).astype(jnp.bfloat16)
    key_rows = rotate(jnp.dot(normed_in, key_master.astype(jnp.bfloat16), preferred_element_type=jnp.float32), places, 0).astype(jnp.bfloat16)
    value_rows = jnp.dot(normed_in, value_master.astype(jnp.bfloat16), preferred_element_type=jnp.float32).astype(jnp.bfloat16)
    gate_rows = jnp.dot(normed_in, swish_master.astype(jnp.bfloat16), preferred_element_type=jnp.float32).astype(jnp.bfloat16)
    running = jnp.cumsum(log_decay.reshape(REQUEST_TOTAL, REQUEST_SPAN, H), axis=1)
    retained = lax.map(retain_prompt, (queries.reshape(REQUEST_TOTAL, REQUEST_SPAN, H, DK), key_rows.reshape(REQUEST_TOTAL, REQUEST_SPAN, H, DK), value_rows.reshape(REQUEST_TOTAL, REQUEST_SPAN, H, DV), running))
    channel_mean = lax.optimization_barrier(jnp.mean(retained, axis=-1, keepdims=True))
    spread = lax.optimization_barrier(jnp.mean(retained * retained, axis=-1, keepdims=True)) - channel_mean * channel_mean
    normed_heads = ((retained - channel_mean) * lax.rsqrt(spread + 1e-05)).reshape(TOKENS, VALS)
    live_rows = places < jnp.repeat(lengths, REQUEST_SPAN)
    gated = jnp.where(live_rows[:, None], jax.nn.silu(gate_rows.astype(jnp.float32)) * normed_heads, 0.0).astype(jnp.bfloat16)
    branch = jnp.dot(gated, output_master.astype(jnp.bfloat16), preferred_element_type=jnp.float32)
    residual = (tokens.astype(jnp.float32) + branch).astype(jnp.bfloat16)
    normed_mid = rms_rows(residual, mlp_gain)
    gate_part = jnp.dot(normed_mid, ffn_gate_master.astype(jnp.bfloat16), preferred_element_type=jnp.float32)
    up_part = jnp.dot(normed_mid, ffn_up_master.astype(jnp.bfloat16), preferred_element_type=jnp.float32)
    hidden = (jax.nn.silu(gate_part) * up_part).astype(jnp.bfloat16)
    return (residual, hidden)
```

```python
import functools
import math

import jax
import jax.numpy as jnp
import numpy as np
from jax import lax
from jax.experimental import pallas as pl
from jax.experimental.pallas import tpu as pltpu
from jax.sharding import PartitionSpec as P

MESH = pl.DeviceIdType.MESH
F32, BF16 = jnp.float32, jnp.bfloat16
D, H, DK, DV = 2048, 8, 256, 512
SPAN, ROWS = 1024, 64
CA, CB = 2048, 1024
VMEM_LIMIT = 64 * 1024 * 1024 - 65536
ANY = pl.BlockSpec(memory_space=pl.ANY)
VM = pl.BlockSpec(memory_space=pltpu.VMEM)


class Spot:
    def __init__(self):
        dp, mp = lax.axis_index("dp"), lax.axis_index("mp")
        self.dp, self.mp = dp, mp
        self.y = lax.div(dp, 4)
        self.c = lax.rem(dp, 2)
        self.z = lax.div(mp, 2)
        self.xl = lax.rem(mp, 2)
        self.xh = lax.rem(lax.div(dp, 2), 2)
        self.x = self.xh * 2 + self.xl
        self.same = self.c == self.xl

    def at_z(self, step):
        z = lax.rem(self.z + (step + 8), 8)
        return z, (self.dp, z * 2 + self.xl)

    def sibling(self):
        return (self.dp + 1 - 2 * self.c, self.mp)

    def partner(self):
        return (self.dp + 1 - 2 * self.c, self.mp + 1 - 2 * self.xl)

    def across(self):
        return (self.dp, self.mp + 1 - 2 * self.xl)

    def plane(self, x, y):
        return (y * 4 + lax.div(x, 2) * 2 + self.c, self.z * 2 + lax.rem(x, 2))


def greet(peers):
    barrier = pltpu.get_barrier_semaphore()
    for peer in peers:
        pl.semaphore_signal(barrier, inc=1, device_id=peer, device_id_type=MESH)
    pl.semaphore_wait(barrier, len(peers))


class Post:
    def __init__(self, sends):
        self.sends, self.count, self.open = sends, 0, []

    def copy(self, src, dst, arrive, peer):
        return pltpu.make_async_remote_copy(
            src_ref=src, dst_ref=dst, send_sem=self.sends.at[self.count], recv_sem=arrive,
            device_id=peer, device_id_type=MESH,
        )

    def send(self, src, dst, arrive, peer):
        made = self.copy(src, dst, arrive, peer)
        self.count += 1
        made.start()
        self.open.append(made)

    def arrived(self, dst, arrive, peer):
        pltpu.make_async_remote_copy(
            src_ref=dst, dst_ref=dst, send_sem=self.sends.at[0], recv_sem=arrive,
            device_id=peer, device_id_type=MESH,
        ).wait_recv()

    def finish(self):
        for made in self.open:
            made.wait_send()


class PlaneGather:
    SENDS, FIRST, SECOND = 4 + 16 + 16, 4, 16

    def __init__(self, spot, post, w, first, second, sib):
        self.s, self.post, self.w = spot, post, w
        self.first, self.second, self.sib = first, second, sib
        c = spot.c
        u, v = (1 - c) * spot.x + c * spot.y, (1 - c) * spot.y + c * spot.x
        ring = lambda a, k: lax.rem(a + (k + 4), 4)
        order = (0, -1, 1, 2)
        self.us, self.vs = [ring(u, k) for k in order], [ring(v, k) for k in order]
        self.sus, self.svs = self.vs, self.us
        self.up, self.um = self.peer(ring(u, 1), v), self.peer(ring(u, -1), v)
        self.vp, self.vm = self.peer(u, ring(v, 1)), self.peer(u, ring(v, -1))

    def xy(self, u, v, c):
        return (1 - c) * u + c * v, (1 - c) * v + c * u

    def peer(self, u, v):
        return self.s.plane(*self.xy(u, v, self.s.c))

    def shard(self, u, v, c, half=None):
        x, y = self.xy(u, v, c)
        dp = y * 4 + lax.div(x, 2) * 2 + c
        rows = pl.ds(0, 8) if half is None else pl.ds(4 * half, 4)
        return self.w.at[dp, rows, lax.rem(x, 2)]

    def mine(self, r, t, half=None):
        return self.shard(self.us[r], self.vs[t], self.s.c, half)

    def neighbours(self):
        return [self.up, self.um, self.vp, self.vm, self.s.sibling()]

    def _go(self, ref, arrive, peer):
        self.post.send(ref, ref, arrive, peer)

    def own(self):
        ref = self.mine(0, 0)
        self._go(ref, self.first.at[0], self.up)
        self._go(ref, self.first.at[1], self.um)
        self._row(0)

    def _row(self, r):
        ref = self.mine(r, 0)
        self._go(ref, self.second.at[4 * r], self.vp)
        self._go(ref, self.second.at[4 * r + 1], self.vm)
        self._go(ref, self.sib.at[4 * r], self.s.sibling())

    def near_first(self):
        self.post.arrived(self.mine(1, 0), self.first.at[0], self.um)
        self._go(self.mine(1, 0, 0), self.first.at[2], self.up)
        self.post.arrived(self.mine(2, 0), self.first.at[1], self.up)
        self._go(self.mine(2, 0, 1), self.first.at[3], self.um)
        self._row(1)
        self._row(2)

    def far_first(self):
        self.post.arrived(self.mine(3, 0, 0), self.first.at[2], self.um)
        self.post.arrived(self.mine(3, 0, 1), self.first.at[3], self.up)
        self._row(3)

    def near_second(self, r):
        self.post.arrived(self.mine(r, 1), self.second.at[4 * r], self.vm)
        self._go(self.mine(r, 1, 0), self.second.at[4 * r + 2], self.vp)
        self.post.arrived(self.mine(r, 2), self.second.at[4 * r + 1], self.vp)
        self._go(self.mine(r, 2, 1), self.second.at[4 * r + 3], self.vm)
        self._go(self.mine(r, 1), self.sib.at[4 * r + 1], self.s.sibling())
        self._go(self.mine(r, 2), self.sib.at[4 * r + 2], self.s.sibling())

    def far_second(self, r):
        self.post.arrived(self.mine(r, 3, 0), self.second.at[4 * r + 2], self.vm)
        self.post.arrived(self.mine(r, 3, 1), self.second.at[4 * r + 3], self.vp)
        self._go(self.mine(r, 3), self.sib.at[4 * r + 3], self.s.sibling())

    def from_sibling(self):
        for r in range(4):
            for t in range(4):
                ref = self.shard(self.sus[r], self.svs[t], 1 - self.s.c)
                self.post.arrived(ref, self.sib.at[4 * r + t], self.s.sibling())


class RingGather:
    SENDS, ARRIVALS = 14, 16

    def __init__(self, spot, post, a, sems):
        self.s, self.post, self.a, self.sems = spot, post, a, sems

    def part(self, step, half):
        z, _ = self.s.at_z(step)
        return self.a.at[z, pl.ds(32 * half, 32)]

    def sem(self, way, step, half):
        return self.sems.at[way * 8 + step * 2 + half]

    def own(self, half, src=None):
        ref = self.part(0, half)
        for way, sign in ((0, 1), (1, -1)):
            self.post.send(ref if src is None else src, ref, self.sem(way, 0, half), self.s.at_z(sign)[1])

    def step(self, k, half):
        for way, sign in ((0, 1), (1, -1)):
            if k == 4 and half != way:
                continue
            ref = self.part(-sign * k, half)
            self.post.arrived(ref, self.sem(way, k - 1, half), self.s.at_z(-sign)[1])
            if k < 3 or (k == 3 and half == way):
                self.post.send(ref, ref, self.sem(way, k, half), self.s.at_z(sign)[1])


def local(src, dst, sem):
    made = pltpu.make_async_copy(src, dst, sem)
    made.start()
    return made


def prep_kernel(tok, gain, decay, length, q, k, v, g, o, fg, fu, nrm, wa, wb, small):
    z = lax.div(lax.axis_index("mp"), 2)
    values = tok[...].astype(F32)
    scale = lax.rsqrt(jnp.mean(values * values, axis=-1, keepdims=True) + 1e-06)
    nrm[...] = (values * scale * gain[...]).astype(BF16)
    for h in range(H):
        wa[h, :, 0:256] = q[:, h * 256 : h * 256 + 256].astype(BF16)
        wa[h, :, 256:512] = k[:, h * 256 : h * 256 + 256].astype(BF16)
        wa[h, :, 512:1024] = v[:, h * 512 : h * 512 + 512].astype(BF16)
        wa[h, :, 1024:1536] = g[:, h * 512 : h * 512 + 512].astype(BF16)
        wa[h, :, 1536:2048] = o[:, h * 512 : h * 512 + 512].astype(BF16)
        wb[h, :, 0:512] = fg[:, h * 512 : h * 512 + 512].astype(BF16)
        wb[h, :, 512:1024] = fu[:, h * 512 : h * 512 + 512].astype(BF16)
    total = decay[...]
    lane = lax.broadcasted_iota(jnp.int32, (H, SPAN), 1)
    reach = 1
    while reach < SPAN:
        total = total + jnp.where(lane >= reach, pltpu.roll(total, reach, 1), 0.0)
        reach *= 2
    row = lax.broadcasted_iota(jnp.int32, (H, SPAN), 0)
    chosen = jnp.sum(jnp.where(row == z, total, 0.0), axis=0, keepdims=True)
    small[...] = jnp.where(row < 4, chosen, length[0, 0])


def prep(*args):
    return pl.pallas_call(
        prep_kernel,
        out_shape=(
            jax.ShapeDtypeStruct((ROWS, D), BF16),
            jax.ShapeDtypeStruct((8, 8, CA), BF16),
            jax.ShapeDtypeStruct((8, 8, CB), BF16),
            jax.ShapeDtypeStruct((8, SPAN), F32),
        ),
        in_specs=[VM] * 3 + [pl.BlockSpec(memory_space=pltpu.SMEM)] + [VM] * 7,
        out_specs=(VM,) * 4,
        name="prep",
    )(*args)


def gather_kernel(nrm, tok, wa, small, acts, tokw, smallw, w, sends, zr, az, p1, p2, ps, misc, lsem):
    s = Spot()
    post = Post(sends)
    plane = PlaneGather(s, post, w, p1, p2, ps)
    greet([s.at_z(k)[1] for k in range(1, 8)] + plane.neighbours() + [s.partner()])

    own = local(wa.at[s.z], w.at[s.dp, s.z, s.xl], lsem.at[0])
    for k in range(1, 8):
        zd, peer = s.at_z(k)
        post.send(wa.at[zd], w.at[s.dp, s.z, s.xl], az.at[k], peer)
    def trade(src, dst, which):
        return pltpu.make_async_remote_copy(
            src_ref=src, dst_ref=dst, send_sem=lsem.at[which], recv_sem=misc.at[which],
            device_id=s.partner(), device_id_type=MESH,
        )

    @pl.when(s.same)
    def _():
        local(nrm, acts.at[s.z], lsem.at[1])
        local(tok, tokw, lsem.at[2])

    @pl.when(jnp.logical_not(s.same))
    def _():
        trade(nrm, acts.at[s.z], 1).start()
        trade(tok, tokw, 2).start()

    post.send(small, smallw, misc.at[0], s.sibling())

    @pl.when(s.same)
    def _():
        pltpu.make_async_copy(nrm, acts.at[s.z], lsem.at[1]).wait()

    @pl.when(jnp.logical_not(s.same))
    def _():
        trade(nrm, acts.at[s.z], 1).wait_recv()

    own.wait()
    for k in range(1, 8):
        zs, peer = s.at_z(-k)
        post.arrived(w.at[s.dp, zs, s.xl], az.at[k], peer)

    ring = RingGather(s, post, acts, zr)
    plane.own()
    ring.own(0)
    ring.own(1)
    plane.near_first()
    ring.step(1, 0)
    ring.step(1, 1)
    plane.far_first()
    plane.near_second(0)
    ring.step(2, 0)
    plane.near_second(1)
    ring.step(2, 1)
    plane.near_second(2)
    plane.far_second(0)
    ring.step(3, 0)
    ring.step(3, 1)
    plane.near_second(3)
    plane.far_second(1)
    plane.far_second(2)
    plane.far_second(3)
    ring.step(4, 0)
    ring.step(4, 1)
    plane.from_sibling()
    post.arrived(smallw, misc.at[0], s.sibling())

    @pl.when(s.same)
    def _():
        pltpu.make_async_copy(tok, tokw, lsem.at[2]).wait()

    @pl.when(jnp.logical_not(s.same))
    def _():
        trade(nrm, acts.at[s.z], 1).wait_send()
        trade(tok, tokw, 2).wait()

    post.finish()


def gather(nrm, tok, wa, small):
    return pl.pallas_call(
        gather_kernel,
        out_shape=(
            jax.ShapeDtypeStruct((8, ROWS, D), BF16),
            jax.ShapeDtypeStruct((ROWS, D), BF16),
            jax.ShapeDtypeStruct((8, SPAN), F32),
            jax.ShapeDtypeStruct((16, 8, 2, 8, CA), BF16),
        ),
        in_specs=[VM] * 4,
        out_specs=(ANY,) * 4,
        scratch_shapes=[
            pltpu.SemaphoreType.DMA((7 + 1 + PlaneGather.SENDS + RingGather.SENDS,)),
            pltpu.SemaphoreType.DMA((16,)),
            pltpu.SemaphoreType.DMA((8,)),
            pltpu.SemaphoreType.DMA((4,)),
            pltpu.SemaphoreType.DMA((16,)),
            pltpu.SemaphoreType.DMA((16,)),
            pltpu.SemaphoreType.DMA((3,)),
            pltpu.SemaphoreType.DMA((4,)),
        ],
        compiler_params=pltpu.CompilerParams(collective_id=0, has_side_effects=True, vmem_limit_bytes=VMEM_LIMIT),
        name="gather",
    )(nrm, tok, wa, small)


def turn_tables():
    frequency = 10000.0 ** (-(np.arange(DK) // 2 * 2) / DK)
    sign = np.where(np.arange(DK) % 2 == 0, -1.0, 1.0)
    far = (np.arange(8) * 128.0)[:, None] * frequency[None]
    near = np.arange(128.0)[:, None] * frequency[None]
    table_far = np.stack([np.cos(far), np.sin(far)]).astype(np.float32)
    table_near = np.stack([np.cos(near), np.sin(near)]).astype(np.float32)
    return table_far, table_near, sign.astype(np.float32)[None]


def head_kernel(
    acts, w, small, smallw, far, near, sign, wb, part, wbp,
    kv, cosine, sine, qs, gs, column, gated, sends, az, misc,
):
    s = Spot()
    post = Post(sends)
    greet([s.at_z(k)[1] for k in range(1, 8)] + [s.sibling()])
    own = local(wb.at[s.z], wbp.at[s.dp, s.z, s.xl], misc.at[0])
    for k in range(1, 8):
        zd, peer = s.at_z(k)
        post.send(wb.at[zd], wbp.at[s.dp, s.z, s.xl], az.at[k], peer)

    base = pl.multiple_of(64 * s.c, 64)
    cn, sn = near[0, pl.ds(base, 64)], near[1, pl.ds(base, 64)]
    for b in range(8):
        cf, sf = far[0, b : b + 1], far[1, b : b + 1]
        cosine[b] = cf * cn - sf * sn
        sine[b] = (sf * cn + cf * sn) * sign[...]
    even = lax.rem(lax.broadcasted_iota(jnp.int32, (256, DK), 1), 2) == 0

    def rot(u, tile):
        c4 = cosine[pl.ds(4 * tile, 4)].reshape(256, DK)
        s4 = sine[pl.ds(4 * tile, 4)].reshape(256, DK)
        swapped = jnp.where(even, pltpu.roll(u, DK - 1, 1), pltpu.roll(u, 1, 1))
        return u * c4 + swapped * s4

    def project(tile, low, width):
        rows = acts[pl.ds(4 * tile, 4)].reshape(256, D)
        return jnp.dot(rows, w[:, low : low + width], preferred_element_type=F32)

    for tile in range(2):
        turned = rot(project(tile, 256, 256), tile).astype(BF16)
        kv[pl.ds(4 * tile, 4), s.c, :, 0:256] = turned.reshape(4, 64, 256)
        values = project(tile, 512, 512).astype(BF16)
        kv[pl.ds(4 * tile, 4), s.c, :, 256:768] = values.reshape(4, 64, 512)
    post.send(kv.at[:, s.c], kv.at[:, s.c], misc.at[1], s.sibling())
    for tile in range(2):
        qs[pl.ds(256 * tile, 256)] = rot(project(tile, 0, 256), tile).astype(BF16)
        gs[pl.ds(256 * tile, 256)] = project(tile, 1024, 512).astype(BF16)
    chosen = jnp.where(s.same, small[...], smallw[...])
    run_row = chosen[0:1]
    length = chosen[4:5, 0:1]
    column[...] = jnp.broadcast_to(run_row, (128, SPAN)).T
    post.arrived(kv.at[:, 1 - s.c], misc.at[1], s.sibling())

    for tile in range(4):
        keys = 256 * (tile + 1)
        q = qs[pl.ds(128 * tile, 128)]
        k = kv[pl.ds(0, 2 * (tile + 1)), :, :, 0:256].reshape(keys, 256)
        v = kv[pl.ds(0, 2 * (tile + 1)), :, :, 256:768].reshape(keys, 512)
        scores = lax.dot_general(q, k, (((1,), (1,)), ((), ())), preferred_element_type=F32) * (DK**-0.5)
        local_row = lax.broadcasted_iota(jnp.int32, (128, 1), 0)
        place = 256 * tile + local_row + jnp.where(local_row >= 64, 64, 0) + 64 * s.c
        at = lax.broadcasted_iota(jnp.int32, (128, keys), 1)
        low = pl.multiple_of(256 * tile + 64 * s.c, 64)
        run_col = jnp.concatenate([column[pl.ds(low, 64), 0:1], column[pl.ds(low + 128, 64), 0:1]], axis=0)
        gap = run_col - run_row[:, :keys]
        weights = (scores * jnp.exp(jnp.where(place >= at, gap, -jnp.inf))).astype(BF16)
        kept = jnp.dot(weights, v, preferred_element_type=F32)
        mean = jnp.mean(kept, axis=-1, keepdims=True)
        spread = jnp.mean(kept * kept, axis=-1, keepdims=True) - mean * mean
        normed = (kept - mean) * lax.rsqrt(spread + 1e-05)
        gate = gs[pl.ds(128 * tile, 128)].astype(F32)
        out = gate / (1.0 + jnp.exp(-gate)) * normed
        live = place.astype(F32) < length
        gated[pl.ds(128 * tile, 128)] = jnp.where(live, out, 0.0).astype(BF16)

    for tile in range(4):
        cols = pl.ds(512 * tile, 512)
        wo = w[cols, 1536:2048]
        out = lax.dot_general(gated[...], wo, (((1,), (1,)), ((), ())), preferred_element_type=F32)
        part[:, :, cols] = out.astype(BF16).reshape(8, 64, 512)

    own.wait()
    for k in range(1, 8):
        zs, peer = s.at_z(-k)
        post.arrived(wbp.at[s.dp, zs, s.xl], az.at[k], peer)
    post.finish()


def head(acts, w, small, smallw, wb):
    far, near, sign = turn_tables()
    return pl.pallas_call(
        head_kernel,
        out_shape=(
            jax.ShapeDtypeStruct((8, ROWS, D), BF16),
            jax.ShapeDtypeStruct((16, 8, 2, 8, CB), BF16),
        ),
        in_specs=[VM] * 8,
        out_specs=(VM, ANY),
        scratch_shapes=[
            pltpu.VMEM((8, 2, ROWS, 768), BF16),
            pltpu.VMEM((8, ROWS, DK), F32),
            pltpu.VMEM((8, ROWS, DK), F32),
            pltpu.VMEM((512, DK), BF16),
            pltpu.VMEM((512, DV), BF16),
            pltpu.VMEM((SPAN, 128), F32),
            pltpu.VMEM((512, DV), BF16),
            pltpu.SemaphoreType.DMA((8,)),
            pltpu.SemaphoreType.DMA((8,)),
            pltpu.SemaphoreType.DMA((2,)),
        ],
        compiler_params=pltpu.CompilerParams(collective_id=1, has_side_effects=True, vmem_limit_bytes=VMEM_LIMIT),
        name="head",
    )(acts, w.reshape(D, CA), small, smallw, far, near, sign, wb)


def middle_kernel(
    part, tokw, gain, wb_in, acts, res, w,
    got, out_box, nbuf, rbuf, sends, rr, zr, p1, p2, ps, misc,
):
    s = Spot()
    post = Post(sends)
    plane = PlaneGather(s, post, w, p1, p2, ps)
    greet([s.at_z(1)[1], s.at_z(-1)[1]] + plane.neighbours() + [s.partner()])

    ways = ((0, 1), (1, -1))

    def rs_send(way, sign, hop, half, src):
        post.send(
            src, got.at[way, hop, pl.ds(32 * half, 32)], rr.at[way * 8 + hop * 2 + half], s.at_z(sign)[1]
        )

    def rs_wait(way, sign, hop, half):
        post.arrived(
            got.at[way, hop, pl.ds(32 * half, 32)], rr.at[way * 8 + hop * 2 + half], s.at_z(-sign)[1]
        )

    def rows(half):
        return pl.ds(32 * half, 32)

    for way, sign in ways:
        rs_send(way, sign, 0, way, part.at[s.at_z(4 * sign)[0], rows(way)])
        rs_send(way, sign, 1, 1 - way, part.at[s.at_z(3 * sign)[0], rows(1 - way)])
    plane.own()

    def relay(hop, half):
        for way, sign in ways:
            if hop == 1 and half != way:
                continue
            rs_wait(way, sign, hop - 1, half)
            here = part[s.at_z((4 - hop) * sign)[0], rows(half)].astype(F32)
            both = here + got[way, hop - 1, rows(half)].astype(F32)
            out_box[way, hop - 1, rows(half)] = both.astype(BF16)
            rs_send(way, sign, hop, half, out_box.at[way, hop - 1, rows(half)])

    relay(1, 0)
    relay(1, 1)
    plane.near_first()
    relay(2, 1)
    relay(2, 0)
    plane.far_first()
    plane.near_second(0)
    relay(3, 1)
    relay(3, 0)
    plane.near_second(1)
    plane.near_second(2)
    plane.far_second(0)

    ring = RingGather(s, post, acts, zr)
    for half in (1, 0):
        for way, sign in ways:
            rs_wait(way, sign, 3, half)
        branch = (
            part[s.z, rows(half)].astype(F32)
            + got[0, 3, rows(half)].astype(F32)
            + got[1, 3, rows(half)].astype(F32)
        )
        residual = (tokw[rows(half)].astype(F32) + branch).astype(BF16)
        rbuf[rows(half)] = residual
        values = residual.astype(F32)
        scale = lax.rsqrt(jnp.mean(values * values, axis=-1, keepdims=True) + 1e-06)
        nbuf[rows(half)] = (values * scale * gain[...]).astype(BF16)
        local(nbuf.at[rows(half)], acts.at[s.z, rows(half)], misc.at[half])
        ring.own(half, nbuf.at[rows(half)])

    slot = post.count
    post.count += 1

    def hand_back():
        return pltpu.make_async_remote_copy(
            src_ref=rbuf, dst_ref=res, send_sem=sends.at[slot], recv_sem=misc.at[2],
            device_id=s.partner(), device_id_type=MESH,
        )

    @pl.when(s.same)
    def _():
        local(rbuf, res, misc.at[3])

    @pl.when(jnp.logical_not(s.same))
    def _():
        hand_back().start()

    plane.near_second(3)
    plane.far_second(1)
    plane.far_second(2)
    ring.step(1, 1)
    ring.step(1, 0)
    plane.far_second(3)
    ring.step(2, 1)
    ring.step(2, 0)
    plane.from_sibling()
    ring.step(3, 1)
    ring.step(3, 0)
    ring.step(4, 1)
    ring.step(4, 0)

    @pl.when(s.same)
    def _():
        pltpu.make_async_copy(rbuf, res, misc.at[3]).wait()

    @pl.when(jnp.logical_not(s.same))
    def _():
        hand_back().wait()

    for half in range(2):
        pltpu.make_async_copy(nbuf.at[rows(half)], acts.at[s.z, rows(half)], misc.at[half]).wait()
    post.finish()


def middle(part, tokw, gain, wb):
    return pl.pallas_call(
        middle_kernel,
        out_shape=(
            jax.ShapeDtypeStruct((8, ROWS, D), BF16),
            jax.ShapeDtypeStruct((ROWS, D), BF16),
            jax.ShapeDtypeStruct((16, 8, 2, 8, CB), BF16),
        ),
        in_specs=[VM] * 3 + [ANY],
        out_specs=(ANY,) * 3,
        input_output_aliases={3: 2},
        scratch_shapes=[
            pltpu.VMEM((2, 4, ROWS, D), BF16),
            pltpu.VMEM((2, 3, ROWS, D), BF16),
            pltpu.VMEM((ROWS, D), BF16),
            pltpu.VMEM((ROWS, D), BF16),
            pltpu.SemaphoreType.DMA((14 + 1 + PlaneGather.SENDS + RingGather.SENDS,)),
            pltpu.SemaphoreType.DMA((16,)),
            pltpu.SemaphoreType.DMA((16,)),
            pltpu.SemaphoreType.DMA((4,)),
            pltpu.SemaphoreType.DMA((16,)),
            pltpu.SemaphoreType.DMA((16,)),
            pltpu.SemaphoreType.DMA((4,)),
        ],
        compiler_params=pltpu.CompilerParams(collective_id=2, has_side_effects=True, vmem_limit_bytes=VMEM_LIMIT),
        name="middle",
    )(part, tokw, gain, wb)


def hidden_kernel(acts, w, out, box, sends, misc):
    s = Spot()
    post = Post(sends)
    greet([s.sibling(), s.across(), s.partner()])

    def half(j, slot):
        for tile in range(2):
            rows = acts[pl.ds(4 * tile, 4)].reshape(256, D)
            low = pl.multiple_of(256 * j, 256)
            gate = jnp.dot(rows, w[:, pl.ds(low, 256)], preferred_element_type=F32)
            up = jnp.dot(rows, w[:, pl.ds(pl.multiple_of(low + 512, 256), 256)], preferred_element_type=F32)
            made = (gate / (1.0 + jnp.exp(-gate)) * up).astype(BF16)
            box[slot, pl.ds(4 * tile, 4)] = made.reshape(4, 64, 256)

    def give(slot, peer, arrive):
        return pltpu.make_async_remote_copy(
            src_ref=box.at[slot], dst_ref=out.at[:, s.c], send_sem=sends.at[slot], recv_sem=misc.at[arrive],
            device_id=peer, device_id_type=MESH,
        )

    half(1 - s.xl, 0)

    @pl.when(s.same)
    def _():
        give(0, s.across(), 0).start()

    @pl.when(jnp.logical_not(s.same))
    def _():
        give(0, s.partner(), 2).start()

    half(s.xl, 1)

    @pl.when(s.same)
    def _():
        kept = local(box.at[1], out.at[:, s.c], misc.at[3])
        kept.wait()
        post.arrived(out.at[:, 1 - s.c], misc.at[1], s.sibling())
        give(0, s.across(), 0).wait_send()

    @pl.when(jnp.logical_not(s.same))
    def _():
        give(1, s.sibling(), 1).start()
        post.arrived(out.at[:, s.c], misc.at[0], s.across())
        post.arrived(out.at[:, 1 - s.c], misc.at[2], s.partner())
        give(0, s.partner(), 2).wait_send()
        give(1, s.sibling(), 1).wait_send()


def hidden(acts, w):
    made = pl.pallas_call(
        hidden_kernel,
        out_shape=jax.ShapeDtypeStruct((8, 2, ROWS, 256), BF16),
        in_specs=[VM] * 2,
        out_specs=ANY,
        scratch_shapes=[
            pltpu.VMEM((2, 8, ROWS, 256), BF16),
            pltpu.SemaphoreType.DMA((2,)),
            pltpu.SemaphoreType.DMA((4,)),
        ],
        compiler_params=pltpu.CompilerParams(collective_id=3, has_side_effects=True, vmem_limit_bytes=VMEM_LIMIT),
        name="hidden",
    )(acts, w.reshape(D, CB))
    return made.reshape(SPAN, 256)


def per_device(tokens, norm_gain, mlp_gain, lengths, log_decay, q, k, v, g, o, fg, fu):
    nrm, wa, wb, small = prep(
        tokens, norm_gain.reshape(1, D), log_decay.T, lengths.astype(F32).reshape(1, 1), q, k, v, g, o.T, fg, fu
    )
    acts, tokw, smallw, w = gather(nrm, tokens, wa, small)
    part, wb = head(acts, w, small, smallw, wb)
    acts, residual, wb = middle(part, tokw, mlp_gain.reshape(1, D), wb)
    return residual, hidden(acts, wb)


def solution(mesh):
    rows = P(("dp", "mp"), None)
    placed = (rows, P(), P(), P("dp"), P("dp", None), rows, rows, rows, rows, P(None, ("dp", "mp")), rows, rows)
    return jax.shard_map(
        per_device, mesh=mesh, in_specs=placed, out_specs=(rows, P("dp", "mp")), check_vma=False
    )
```

```python
import functools
import math

import jax
import jax.numpy as jnp
import numpy as np
from jax import lax
from jax.experimental import pallas as pl
from jax.experimental.pallas import tpu as pltpu
from jax.sharding import PartitionSpec as P

MESH = pl.DeviceIdType.MESH
F32, BF16 = jnp.float32, jnp.bfloat16
D, H, DK, DV = 2048, 8, 256, 512
SPAN, ROWS = 1024, 64
CA, CB = 2048, 1024
VMEM_LIMIT = 64 * 1024 * 1024 - 65536
ANY = pl.BlockSpec(memory_space=pl.ANY)
SM = pl.BlockSpec(memory_space=pltpu.SMEM)
VM = pl.BlockSpec(memory_space=pltpu.VMEM)


class Spot:
    def __init__(self):
        dp, mp = lax.axis_index("dp"), lax.axis_index("mp")
        self.dp, self.mp = dp, mp
        self.y = lax.div(dp, 4)
        self.c = lax.rem(dp, 2)
        self.z = lax.div(mp, 2)
        self.xl = lax.rem(mp, 2)
        self.xh = lax.rem(lax.div(dp, 2), 2)
        self.x = self.xh * 2 + self.xl
        self.same = self.c == self.xl

    def at_z(self, step):
        z = lax.rem(self.z + (step + 8), 8)
        return z, (self.dp, z * 2 + self.xl)

    def sibling(self):
        return (self.dp + 1 - 2 * self.c, self.mp)

    def partner(self):
        return (self.dp + 1 - 2 * self.c, self.mp + 1 - 2 * self.xl)

    def across(self):
        return (self.dp, self.mp + 1 - 2 * self.xl)

    def plane(self, x, y):
        return (y * 4 + lax.div(x, 2) * 2 + self.c, self.z * 2 + lax.rem(x, 2))


class Post:
    def __init__(self, sends):
        self.sends, self.count, self.open = sends, 0, []

    def copy(self, src, dst, arrive, peer):
        return pltpu.make_async_remote_copy(
            src_ref=src, dst_ref=dst, send_sem=self.sends.at[self.count], recv_sem=arrive,
            device_id=peer, device_id_type=MESH,
        )

    def send(self, src, dst, arrive, peer):
        made = self.copy(src, dst, arrive, peer)
        self.count += 1
        made.start()
        self.open.append(made)

    def arrived(self, dst, arrive, peer):
        pltpu.make_async_remote_copy(
            src_ref=dst, dst_ref=dst, send_sem=self.sends.at[0], recv_sem=arrive,
            device_id=peer, device_id_type=MESH,
        ).wait_recv()

    def finish(self):
        for made in self.open:
            made.wait_send()


class PlaneGather:
    SENDS, FIRST, SECOND = 4 + 16 + 16, 4, 16

    def __init__(self, spot, post, w, cols, first, second, sib):
        self.s, self.post, self.w, self.cols = spot, post, w, cols
        self.first, self.second, self.sib = first, second, sib
        c = spot.c
        u, v = (1 - c) * spot.x + c * spot.y, (1 - c) * spot.y + c * spot.x
        ring = lambda a, k: lax.rem(a + (k + 4), 4)
        order = (0, -1, 1, 2)
        self.us, self.vs = [ring(u, k) for k in order], [ring(v, k) for k in order]
        self.sus, self.svs = self.vs, self.us
        self.up, self.um = self.peer(ring(u, 1), v), self.peer(ring(u, -1), v)
        self.vp, self.vm = self.peer(u, ring(v, 1)), self.peer(u, ring(v, -1))

    def xy(self, u, v, c):
        return (1 - c) * u + c * v, (1 - c) * v + c * u

    def peer(self, u, v):
        return self.s.plane(*self.xy(u, v, self.s.c))

    def shard(self, u, v, c, half=None):
        x, y = self.xy(u, v, c)
        dp = y * 4 + lax.div(x, 2) * 2 + c
        rows = pl.ds(0, 8) if half is None else pl.ds(4 * half, 4)
        return self.w.at[dp, rows, lax.rem(x, 2), :, self.cols]

    def mine(self, r, t, half=None):
        return self.shard(self.us[r], self.vs[t], self.s.c, half)

    def neighbours(self):
        return [self.up, self.um, self.vp, self.vm, self.s.sibling()]

    def _go(self, ref, arrive, peer):
        self.post.send(ref, ref, arrive, peer)

    def own(self):
        ref = self.mine(0, 0)
        self._go(ref, self.first.at[0], self.up)
        self._go(ref, self.first.at[1], self.um)
        self._row(0)

    def _row(self, r):
        ref = self.mine(r, 0)
        self._go(ref, self.second.at[4 * r], self.vp)
        self._go(ref, self.second.at[4 * r + 1], self.vm)
        self._go(ref, self.sib.at[4 * r], self.s.sibling())

    def near_first(self):
        self.post.arrived(self.mine(1, 0), self.first.at[0], self.um)
        self._go(self.mine(1, 0, 0), self.first.at[2], self.up)
        self.post.arrived(self.mine(2, 0), self.first.at[1], self.up)
        self._go(self.mine(2, 0, 1), self.first.at[3], self.um)
        self._row(1)
        self._row(2)

    def far_first(self):
        self.post.arrived(self.mine(3, 0, 0), self.first.at[2], self.um)
        self.post.arrived(self.mine(3, 0, 1), self.first.at[3], self.up)
        self._row(3)

    def near_second(self, r):
        self.post.arrived(self.mine(r, 1), self.second.at[4 * r], self.vm)
        self._go(self.mine(r, 1, 0), self.second.at[4 * r + 2], self.vp)
        self.post.arrived(self.mine(r, 2), self.second.at[4 * r + 1], self.vp)
        self._go(self.mine(r, 2, 1), self.second.at[4 * r + 3], self.vm)
        self._go(self.mine(r, 1), self.sib.at[4 * r + 1], self.s.sibling())
        self._go(self.mine(r, 2), self.sib.at[4 * r + 2], self.s.sibling())

    def far_second(self, r):
        self.post.arrived(self.mine(r, 3, 0), self.second.at[4 * r + 2], self.vm)
        self.post.arrived(self.mine(r, 3, 1), self.second.at[4 * r + 3], self.vp)
        self._go(self.mine(r, 3), self.sib.at[4 * r + 3], self.s.sibling())

    def from_sibling(self):
        for r in range(4):
            for t in range(4):
                ref = self.shard(self.sus[r], self.svs[t], 1 - self.s.c)
                self.post.arrived(ref, self.sib.at[4 * r + t], self.s.sibling())


def slot_of(r):
    return (r + 2) % 8


NEAR, FAR = (0, 5), (5, 3)


class RingGather:
    SENDS, ARRIVALS = 14, 16

    def __init__(self, spot, post, a, sems):
        self.s, self.post, self.a, self.sems = spot, post, a, sems

    def part(self, r, half):
        return self.a.at[slot_of(r), pl.ds(32 * half, 32)]

    def sem(self, way, step, half):
        return self.sems.at[way * 8 + step * 2 + half]

    def own(self, half):
        for way, sign in ((0, 1), (1, -1)):
            self.post.send(self.part(0, half), self.part(-sign, half), self.sem(way, 0, half), self.s.at_z(sign)[1])

    def step(self, k, half):
        for way, sign in ((0, 1), (1, -1)):
            if k == 4 and half != way:
                continue
            ref = self.part(-sign * k, half)
            self.post.arrived(ref, self.sem(way, k - 1, half), self.s.at_z(-sign)[1])
            if k < 3 or (k == 3 and half == way):
                self.post.send(ref, self.part(-sign * (k + 1), half), self.sem(way, k, half), self.s.at_z(sign)[1])


def local(src, dst, sem):
    made = pltpu.make_async_copy(src, dst, sem)
    made.start()
    return made


def turn_tables():
    frequency = 10000.0 ** (-(np.arange(DK) // 2 * 2) / DK)
    sign = np.where(np.arange(DK) % 2 == 0, -1.0, 1.0)
    far = (np.arange(8) * 128.0)[:, None] * frequency[None]
    near = np.arange(128.0)[:, None] * frequency[None]
    table_far = np.stack([np.cos(far), np.sin(far)]).astype(np.float32)
    table_near = np.stack([np.cos(near), np.sin(near)]).astype(np.float32)
    return table_far, table_near, sign.astype(np.float32)[None]


def rms(values, gain):
    scale = lax.rsqrt(jnp.mean(values * values, axis=-1, keepdims=True) + 1e-06)
    return (values * scale * gain).astype(BF16)


def silu(v):
    return v / (1.0 + jnp.exp(-v))


def layer_kernel(
    tok, gain, mlp_gain, decay, length, q, k, v, g, o, fg, fu, far, near, sign,
    res, hid,
    wa, wb, nrm, small, smallw, tokw, wao, wbb, acts, acts2, kv, cosine, sine, qs, gs, runs, column, gated,
    part, got, out_box, rbuf, box,
    sends, za, zb, zr1, zr2, rr, pa1, pa2, pa3, po1, po2, po3, pb1, pb2, pb3, misc, lsem, hsend, hx, hp, hs,
):
    s = Spot()
    post = Post(sends)
    plane_a = PlaneGather(s, post, wao, pl.ds(0, 1536), pa1, pa2, pa3)
    plane_o = PlaneGather(s, post, wao, pl.ds(1536, 512), po1, po2, po3)
    plane_b = PlaneGather(s, post, wbb, pl.ds(0, CB), pb1, pb2, pb3)
    ring1, ring2 = RingGather(s, post, acts, zr1), RingGather(s, post, acts2, zr2)
    barrier = pltpu.get_barrier_semaphore()
    peers = [s.at_z(n)[1] for n in range(1, 8)] + plane_a.neighbours() + [s.partner()]
    for peer in peers:
        pl.semaphore_signal(barrier, inc=1, device_id=peer, device_id_type=MESH)

    for h in range(H):
        wa[h, :, 0:256] = q[:, h * 256 : h * 256 + 256].astype(BF16)
        wa[h, :, 256:512] = k[:, h * 256 : h * 256 + 256].astype(BF16)
        wa[h, :, 512:1024] = v[:, h * 512 : h * 512 + 512].astype(BF16)
        wa[h, :, 1024:1536] = g[:, h * 512 : h * 512 + 512].astype(BF16)
        wa[h, :, 1536:2048] = o[:, h * 512 : h * 512 + 512].astype(BF16)
        wb[h, :, 0:512] = fg[:, h * 512 : h * 512 + 512].astype(BF16)
        wb[h, :, 512:1024] = fu[:, h * 512 : h * 512 + 512].astype(BF16)
    nrm[...] = rms(tok[...].astype(F32), gain[...])
    total = decay[...]
    lane = lax.broadcasted_iota(jnp.int32, (H, SPAN), 1)
    reach = 1
    while reach < SPAN:
        total = total + jnp.where(lane >= reach, pltpu.roll(total, reach, 1), 0.0)
        reach *= 2
    row = lax.broadcasted_iota(jnp.int32, (H, SPAN), 0)
    chosen = jnp.sum(jnp.where(row == s.z, total, 0.0), axis=0, keepdims=True)
    small[...] = jnp.where(row < 4, chosen, length[0, 0])

    pl.semaphore_wait(barrier, len(peers))

    def trade(src, dst, which):
        return pltpu.make_async_remote_copy(
            src_ref=src, dst_ref=dst, send_sem=lsem.at[which], recv_sem=misc.at[which],
            device_id=s.partner(), device_id_type=MESH,
        )

    own_a = local(wa.at[s.z], wao.at[s.dp, s.z, s.xl], lsem.at[0])
    own_b = local(wb.at[s.z], wbb.at[s.dp, s.z, s.xl], lsem.at[3])

    @pl.when(jnp.logical_not(s.same))
    def _():
        trade(nrm, acts.at[slot_of(0)], 1).start()
        trade(tok, tokw, 2).start()

    @pl.when(s.same)
    def _():
        local(nrm, acts.at[slot_of(0)], lsem.at[1])
        local(tok, tokw, lsem.at[2])

    for n in (4, 3, 5, 2, 6, 1, 7):
        zd, peer = s.at_z(n)
        post.send(wa.at[zd], wao.at[s.dp, s.z, s.xl], za.at[n], peer)
    post.send(small, smallw, misc.at[0], s.sibling())

    base = pl.multiple_of(64 * s.c, 64)
    cn, sn = near[0, pl.ds(base, 64)], near[1, pl.ds(base, 64)]
    for i in range(8):
        b, _ = s.at_z(i - 2)
        cf, sf = far[0, pl.ds(b, 1)], far[1, pl.ds(b, 1)]
        cosine[i] = cf * cn - sf * sn
        sine[i] = (sf * cn + cf * sn) * sign[...]

    @pl.when(s.same)
    def _():
        pltpu.make_async_copy(nrm, acts.at[slot_of(0)], lsem.at[1]).wait()

    @pl.when(jnp.logical_not(s.same))
    def _():
        trade(nrm, acts.at[slot_of(0)], 1).wait_recv()

    own_a.wait()
    for n in range(1, 8):
        zs, peer = s.at_z(-n)
        post.arrived(wao.at[s.dp, zs, s.xl], za.at[n], peer)

    plane_a.own()
    ring1.own(0)
    ring1.own(1)

    post.arrived(smallw, misc.at[0], s.sibling())
    runs[...] = jnp.where(s.same, small[...], smallw[...])
    pieces = [runs[0:1, pl.ds(pl.multiple_of(128 * s.at_z(i - 2)[0], 128), 128)] for i in range(8)]
    run_row = jnp.concatenate(pieces, axis=1)
    column[...] = jnp.broadcast_to(run_row, (128, SPAN)).T
    last = runs[4:5, 0:1]
    at = lax.rem(lax.broadcasted_iota(jnp.int32, (1, SPAN), 1) + 128 * (s.z + 6), SPAN)

    plane_a.near_first()
    plane_o.own()
    ring1.step(1, 0)
    ring1.step(1, 1)
    plane_a.far_first()
    plane_a.near_second(0)
    ring1.step(2, 0)
    plane_a.near_second(1)
    plane_o.near_first()
    ring1.step(2, 1)
    plane_a.near_second(2)
    plane_a.far_second(0)
    ring1.step(3, 0)
    plane_o.far_first()
    plane_a.near_second(3)
    plane_a.far_second(1)
    ring1.step(3, 1)
    plane_a.far_second(2)
    plane_a.far_second(3)
    plane_a.from_sibling()

    weights_a = wao.reshape(D, CA)
    weights_b = wbb.reshape(D, CB)

    def project(span, low, width):
        first, count = span
        rows = acts[first : first + count].reshape(64 * count, D)
        return jnp.dot(rows, weights_a[:, low : low + width], preferred_element_type=F32)

    def rot(u, span):
        first, count = span
        n = 64 * count
        even = lax.rem(lax.broadcasted_iota(jnp.int32, (n, DK), 1), 2) == 0
        swapped = jnp.where(even, pltpu.roll(u, DK - 1, 1), pltpu.roll(u, 1, 1))
        turned = u * cosine[first : first + count].reshape(n, DK) + swapped * sine[first : first + count].reshape(n, DK)
        return turned.astype(BF16)

    def key_part(span):
        first, count = span
        kv[first : first + count, s.c, :, 0:256] = rot(project(span, 256, 256), span).reshape(count, 64, 256)

    def value_part(span, which):
        first, count = span
        made = project(span, 512 + 256 * which, 256).astype(BF16).reshape(count, 64, 256)
        kv[first : first + count, s.c, :, 256 + 256 * which : 512 + 256 * which] = made

    def query_part(span):
        first, count = span
        qs[64 * first : 64 * (first + count)] = rot(project(span, 0, 256), span)

    def gate_part(span, which):
        first, count = span
        made = project(span, 1024 + 256 * which, 256).astype(BF16)
        gs[64 * first : 64 * (first + count), 256 * which : 256 * which + 256] = made

    def share(span, arrive):
        mine = kv.at[pl.ds(*span), s.c]
        post.send(mine, mine, arrive, s.sibling())

    def shared(span, arrive):
        post.arrived(kv.at[pl.ds(*span), 1 - s.c], arrive, s.sibling())

    def retain(span):
        first, count = span
        n = 64 * count
        rows = slice(64 * first, 64 * (first + count))
        keys = kv[:, :, :, 0:256].reshape(SPAN, 256)
        values = kv[:, :, :, 256:768].reshape(SPAN, 512)
        scores = lax.dot_general(qs[rows], keys, (((1,), (1,)), ((), ())), preferred_element_type=F32) * (DK**-0.5)
        step = lax.broadcasted_iota(jnp.int32, (n, 1), 0)
        block = lax.div(step, 64)
        place = 128 * lax.rem(block + (s.z + first + 6), 8) + 64 * s.c + (step - 64 * block)
        run_col = jnp.concatenate(
            [column[pl.ds(pl.multiple_of(128 * i + 64 * s.c, 64), 64), 0:1] for i in range(first, first + count)], axis=0
        )
        weights = (scores * jnp.exp(jnp.where(place >= at, run_col - run_row, -jnp.inf))).astype(BF16)
        kept = jnp.dot(weights, values, preferred_element_type=F32)
        mean = jnp.mean(kept, axis=-1, keepdims=True)
        spread = jnp.mean(kept * kept, axis=-1, keepdims=True) - mean * mean
        normed = (kept - mean) * lax.rsqrt(spread + 1e-05)
        live = place.astype(F32) < last
        gated[rows] = jnp.where(live, silu(gs[rows].astype(F32)) * normed, 0.0).astype(BF16)

    def put_out(span):
        first, count = span
        rows = slice(64 * first, 64 * (first + count))
        for tile in range(4):
            wo = weights_a[512 * tile : 512 * tile + 512, 1536:2048]
            made = lax.dot_general(gated[rows], wo, (((1,), (1,)), ((), ())), preferred_element_type=F32)
            part[first : first + count, :, 512 * tile : 512 * tile + 512] = made.astype(BF16).reshape(count, 64, 512)

    key_part(NEAR)
    plane_o.near_second(0)
    value_part(NEAR, 0)
    plane_o.near_second(1)
    value_part(NEAR, 1)
    share(NEAR, misc.at[3])
    ring1.step(4, 0)
    ring1.step(4, 1)
    plane_o.near_second(2)
    plane_o.far_second(0)
    for n in (4, 3, 5, 2, 6, 1, 7):
        zd, peer = s.at_z(n)
        post.send(wb.at[zd], wbb.at[s.dp, s.z, s.xl], zb.at[n], peer)
    key_part(FAR)
    value_part(FAR, 0)
    value_part(FAR, 1)
    share(FAR, misc.at[4])
    plane_o.near_second(3)
    plane_o.far_second(1)
    plane_o.far_second(2)
    query_part(FAR)
    gate_part(FAR, 0)
    gate_part(FAR, 1)
    plane_o.far_second(3)
    shared(NEAR, misc.at[3])
    shared(FAR, misc.at[4])
    retain(FAR)
    plane_o.from_sibling()
    put_out(FAR)

    ways = ((0, 1), (1, -1))

    def rows(half):
        return pl.ds(32 * half, 32)

    def rs_send(way, sign, hop, half, src):
        post.send(src, got.at[way, hop, rows(half)], rr.at[way * 8 + hop * 2 + half], s.at_z(sign)[1])

    def rs_wait(way, sign, hop, half):
        post.arrived(got.at[way, hop, rows(half)], rr.at[way * 8 + hop * 2 + half], s.at_z(-sign)[1])

    def relay(hop, half):
        for way, sign in ways:
            if hop == 1 and half != way:
                continue
            rs_wait(way, sign, hop - 1, half)
            here = part[slot_of((4 - hop) * sign), rows(half)].astype(F32)
            both = here + got[way, hop - 1, rows(half)].astype(F32)
            out_box[way, hop - 1, rows(half)] = both.astype(BF16)
            rs_send(way, sign, hop, half, out_box.at[way, hop - 1, rows(half)])

    for way, sign in ways:
        rs_send(way, sign, 0, way, part.at[slot_of(4), rows(way)])
        rs_send(way, sign, 1, 1 - way, part.at[slot_of(3 * sign), rows(1 - way)])
    own_b.wait()
    for n in range(1, 8):
        zs, peer = s.at_z(-n)
        post.arrived(wbb.at[s.dp, zs, s.xl], zb.at[n], peer)
    plane_b.own()
    query_part(NEAR)
    gate_part(NEAR, 0)
    gate_part(NEAR, 1)
    relay(1, 0)
    relay(1, 1)
    retain(NEAR)
    plane_b.near_first()
    put_out(NEAR)
    relay(2, 1)
    relay(2, 0)
    plane_b.far_first()
    plane_b.near_second(0)
    relay(3, 1)
    relay(3, 0)
    plane_b.near_second(1)
    plane_b.near_second(2)
    plane_b.far_second(0)

    for half in (1, 0):
        for way, sign in ways:
            rs_wait(way, sign, 3, half)
        branch = (
            part[slot_of(0), rows(half)].astype(F32)
            + got[0, 3, rows(half)].astype(F32)
            + got[1, 3, rows(half)].astype(F32)
        )
        residual = (tokw_ready(s, trade, tok, tokw, lsem, half)[rows(half)].astype(F32) + branch).astype(BF16)
        rbuf[rows(half)] = residual
        acts2[slot_of(0), rows(half)] = rms(residual.astype(F32), mlp_gain[...])
        ring2.own(half)

    def hand_back():
        return pltpu.make_async_remote_copy(
            src_ref=rbuf, dst_ref=res, send_sem=lsem.at[4], recv_sem=misc.at[5],
            device_id=s.partner(), device_id_type=MESH,
        )

    @pl.when(s.same)
    def _():
        local(rbuf, res, lsem.at[4])

    @pl.when(jnp.logical_not(s.same))
    def _():
        hand_back().start()

    def hide(span, j, slot):
        first, count = span
        low = pl.multiple_of(256 * j, 256)
        high = pl.multiple_of(256 * j + 512, 256)
        rows2 = acts2[first : first + count].reshape(64 * count, D)
        gate = jnp.dot(rows2, weights_b[:, pl.ds(low, 256)], preferred_element_type=F32)
        up = jnp.dot(rows2, weights_b[:, pl.ds(high, 256)], preferred_element_type=F32)
        box[slot, first : first + count] = (silu(gate) * up).astype(BF16).reshape(count, 64, 256)

    def give(slot, i, peer, arrive):
        b, _ = s.at_z(i - 2)
        return pltpu.make_async_remote_copy(
            src_ref=box.at[slot, i], dst_ref=hid.at[b, s.c], send_sem=hsend.at[8 * slot + i], recv_sem=arrive.at[i],
            device_id=peer, device_id_type=MESH,
        )

    def keep(i):
        b, _ = s.at_z(i - 2)
        return pltpu.make_async_copy(box.at[1, i], hid.at[b, s.c], hsend.at[8 + i])

    def give_far(span):
        first, count = span

        @pl.when(s.same)
        def _():
            for i in range(first, first + count):
                give(0, i, s.across(), hx).start()

        @pl.when(jnp.logical_not(s.same))
        def _():
            for i in range(first, first + count):
                give(0, i, s.partner(), hp).start()

    def give_near(span):
        first, count = span

        @pl.when(s.same)
        def _():
            for i in range(first, first + count):
                keep(i).start()

        @pl.when(jnp.logical_not(s.same))
        def _():
            for i in range(first, first + count):
                give(1, i, s.sibling(), hs).start()

    plane_b.near_second(3)
    plane_b.far_second(1)
    plane_b.far_second(2)
    ring2.step(1, 1)
    ring2.step(1, 0)
    plane_b.far_second(3)
    ring2.step(2, 1)
    ring2.step(2, 0)
    plane_b.from_sibling()
    hide(NEAR, 1 - s.xl, 0)
    give_far(NEAR)
    ring2.step(3, 1)
    ring2.step(3, 0)
    hide(NEAR, s.xl, 1)
    give_near(NEAR)
    ring2.step(4, 1)
    ring2.step(4, 0)
    hide(FAR, 1 - s.xl, 0)
    give_far(FAR)
    hide(FAR, s.xl, 1)
    give_near(FAR)

    @pl.when(s.same)
    def _():
        pltpu.make_async_copy(rbuf, res, lsem.at[4]).wait()
        for i in range(8):
            keep(i).wait()
            give(0, i, s.across(), hx).wait_send()
            b, _ = s.at_z(i - 2)
            post.arrived(hid.at[b, 1 - s.c], hs.at[i], s.sibling())

    @pl.when(jnp.logical_not(s.same))
    def _():
        hand_back().wait()
        trade(nrm, acts.at[slot_of(0)], 1).wait_send()
        trade(tok, tokw, 2).wait_send()
        for i in range(8):
            give(0, i, s.partner(), hp).wait_send()
            give(1, i, s.sibling(), hs).wait_send()
            b, _ = s.at_z(i - 2)
            post.arrived(hid.at[b, s.c], hx.at[i], s.across())
            post.arrived(hid.at[b, 1 - s.c], hp.at[i], s.partner())

    post.finish()


def tokw_ready(s, trade, tok, tokw, lsem, half):
    if half == 1:

        @pl.when(s.same)
        def _():
            pltpu.make_async_copy(tok, tokw, lsem.at[2]).wait()

        @pl.when(jnp.logical_not(s.same))
        def _():
            trade(tok, tokw, 2).wait_recv()

    return tokw


def layer(*args):
    dma = lambda n: pltpu.SemaphoreType.DMA((n,))
    plane_sems = [dma(4), dma(16), dma(16)]
    sends = 7 + 7 + 1 + 2 + 14 + 2 * RingGather.SENDS + 3 * PlaneGather.SENDS
    return pl.pallas_call(
        layer_kernel,
        out_shape=(jax.ShapeDtypeStruct((ROWS, D), BF16), jax.ShapeDtypeStruct((8, 2, ROWS, 256), BF16)),
        in_specs=[VM] * 4 + [SM] + [VM] * 10,
        out_specs=(ANY, ANY),
        scratch_shapes=[
            pltpu.VMEM((8, 8, CA), BF16),
            pltpu.VMEM((8, 8, CB), BF16),
            pltpu.VMEM((ROWS, D), BF16),
            pltpu.VMEM((8, SPAN), F32),
            pltpu.VMEM((8, SPAN), F32),
            pltpu.VMEM((ROWS, D), BF16),
            pltpu.VMEM((16, 8, 2, 8, CA), BF16),
            pltpu.VMEM((16, 8, 2, 8, CB), BF16),
            pltpu.VMEM((8, ROWS, D), BF16),
            pltpu.VMEM((8, ROWS, D), BF16),
            pltpu.VMEM((8, 2, ROWS, 768), BF16),
            pltpu.VMEM((8, ROWS, DK), F32),
            pltpu.VMEM((8, ROWS, DK), F32),
            pltpu.VMEM((512, DK), BF16),
            pltpu.VMEM((512, DV), BF16),
            pltpu.VMEM((8, SPAN), F32),
            pltpu.VMEM((SPAN, 128), F32),
            pltpu.VMEM((512, DV), BF16),
            pltpu.VMEM((8, ROWS, D), BF16),
            pltpu.VMEM((2, 4, ROWS, D), BF16),
            pltpu.VMEM((2, 3, ROWS, D), BF16),
            pltpu.VMEM((ROWS, D), BF16),
            pltpu.VMEM((2, 8, ROWS, 256), BF16),
            dma(sends), dma(8), dma(8), dma(16), dma(16), dma(16),
            *plane_sems, *plane_sems, *plane_sems,
            dma(6), dma(5), dma(16), dma(8), dma(8), dma(8),
        ],
        compiler_params=pltpu.CompilerParams(collective_id=0, has_side_effects=True, vmem_limit_bytes=VMEM_LIMIT),
        name="layer",
    )(*args)


def finish_kernel(res, hid, res_out, hid_out):
    res_out[...] = res[...]
    hid_out[...] = hid[...]


def finish(res, hid):
    return pl.pallas_call(
        finish_kernel,
        out_shape=(jax.ShapeDtypeStruct(res.shape, BF16), jax.ShapeDtypeStruct(hid.shape, BF16)),
        in_specs=[VM] * 2,
        out_specs=(VM, VM),
        name="finish",
    )(res, hid)


def per_device(tokens, norm_gain, mlp_gain, lengths, log_decay, q, k, v, g, o, fg, fu):
    far, near, sign = turn_tables()
    res, hid = layer(
        tokens, norm_gain.reshape(1, D), mlp_gain.reshape(1, D), log_decay.T, lengths.astype(F32).reshape(1, 1),
        q, k, v, g, o.T, fg, fu, far, near, sign,
    )
    return finish(res, hid.reshape(SPAN, 256))


def solution(mesh):
    rows = P(("dp", "mp"), None)
    placed = (rows, P(), P(), P("dp"), P("dp", None), rows, rows, rows, rows, P(None, ("dp", "mp")), rows, rows)
    return jax.shard_map(
        per_device, mesh=mesh, in_specs=placed, out_specs=(rows, P("dp", "mp")), check_vma=False
    )
```

```python
import functools
import math

import jax
import jax.numpy as jnp
import numpy as np
from jax import lax
from jax.experimental import pallas as pl
from jax.experimental.pallas import tpu as pltpu
from jax.sharding import PartitionSpec as P

MESH = pl.DeviceIdType.MESH
F32, BF16 = jnp.float32, jnp.bfloat16
D, H, DK, DV = 2048, 8, 256, 512
SPAN, ROWS = 1024, 64
CA, CB = 2048, 1024
VMEM_LIMIT = 64 * 1024 * 1024 - 65536
ANY = pl.BlockSpec(memory_space=pl.ANY)
SM = pl.BlockSpec(memory_space=pltpu.SMEM)
VM = pl.BlockSpec(memory_space=pltpu.VMEM)


class Spot:
    def __init__(self):
        dp, mp = lax.axis_index("dp"), lax.axis_index("mp")
        self.dp, self.mp = dp, mp
        self.y = lax.div(dp, 4)
        self.c = lax.rem(dp, 2)
        self.z = lax.div(mp, 2)
        self.xl = lax.rem(mp, 2)
        self.xh = lax.rem(lax.div(dp, 2), 2)
        self.x = self.xh * 2 + self.xl
        self.same = self.c == self.xl

    def at_z(self, step):
        z = lax.rem(self.z + (step + 8), 8)
        return z, (self.dp, z * 2 + self.xl)

    def sibling(self):
        return (self.dp + 1 - 2 * self.c, self.mp)

    def partner(self):
        return (self.dp + 1 - 2 * self.c, self.mp + 1 - 2 * self.xl)

    def across(self):
        return (self.dp, self.mp + 1 - 2 * self.xl)

    def plane(self, x, y):
        return (y * 4 + lax.div(x, 2) * 2 + self.c, self.z * 2 + lax.rem(x, 2))


class Post:
    def copy(self, src, dst, arrive, peer, done):
        return pltpu.make_async_remote_copy(
            src_ref=src, dst_ref=dst, send_sem=done, recv_sem=arrive, device_id=peer, device_id_type=MESH
        )

    def send(self, src, dst, arrive, peer, done):
        self.copy(src, dst, arrive, peer, done).start()

    def arrived(self, ref, arrive, peer):
        self.copy(ref, ref, arrive, peer, arrive).wait_recv()

    def sent(self, ref, done, peer):
        self.copy(ref, ref, done, peer, done).wait_send()


class PlaneGather:
    FIRST, SECOND, ENDS = 4, 12, 4

    def __init__(self, spot, post, w, cols, way, first, second, ends):
        self.s, self.post, self.w, self.cols, self.way = spot, post, w, cols, way
        self.first, self.second, self.ends = first, second, ends
        u, v = (spot.y, spot.x) if way else (spot.x, spot.y)
        ring = lambda a, k: lax.rem(a + (k + 4), 4)
        order = (0, -1, 1, 2)
        self.us, self.vs = [ring(u, k) for k in order], [ring(v, k) for k in order]
        self.up, self.um = self.peer(ring(u, 1), v), self.peer(ring(u, -1), v)
        self.vp, self.vm = self.peer(u, ring(v, 1)), self.peer(u, ring(v, -1))

    def xy(self, u, v):
        return (v, u) if self.way else (u, v)

    def peer(self, u, v):
        return self.s.plane(*self.xy(u, v))

    def rows(self, half):
        return pl.ds(4 * self.way, 4) if half is None else pl.ds(4 * self.way + 2 * half, 2)

    def mine(self, r, t, half=None):
        x, y = self.xy(self.us[r], self.vs[t])
        return self.w.at[y, lax.div(x, 2), self.s.c, self.rows(half), lax.rem(x, 2), :, self.cols]

    def group(self, t):
        v, c, rows = self.vs[t], self.s.c, self.rows(None)
        if self.way:
            return self.w.at[:, lax.div(v, 2), c, rows, lax.rem(v, 2), :, self.cols]
        return self.w.at[v, :, c, rows, :, :, self.cols]

    def neighbours(self):
        return [self.up, self.um, self.vp, self.vm, self.s.sibling()]

    def _go(self, ref, arrive, peer, end):
        self.post.send(ref, ref, arrive, peer, self.ends.at[end])

    def _over(self, ref):
        self._go(ref, self.ends.at[3], self.s.sibling(), 2)

    def own(self):
        ref = self.mine(0, 0)
        self._go(ref, self.first.at[0], self.up, 0)
        self._go(ref, self.first.at[1], self.um, 0)
        self._row(0)

    def _row(self, r):
        ref = self.mine(r, 0)
        self._go(ref, self.second.at[3 * r], self.vp, 1)
        self._go(ref, self.second.at[3 * r + 1], self.vm, 1)

    def near_first(self):
        self.post.arrived(self.mine(1, 0), self.first.at[0], self.um)
        self._go(self.mine(1, 0, 0), self.first.at[2], self.up, 0)
        self.post.arrived(self.mine(2, 0), self.first.at[1], self.up)
        self._go(self.mine(2, 0, 1), self.first.at[3], self.um, 0)
        self._row(1)
        self._row(2)

    def far_first(self):
        self.post.arrived(self.mine(3, 0, 0), self.first.at[2], self.um)
        self.post.arrived(self.mine(3, 0, 1), self.first.at[3], self.up)
        self._row(3)
        self._over(self.group(0))

    def near_second(self, r):
        self.post.arrived(self.mine(r, 1), self.second.at[3 * r], self.vm)
        if r < 2:
            self._go(self.mine(r, 1), self.second.at[3 * r + 2], self.vp, 1)
        self.post.arrived(self.mine(r, 2), self.second.at[3 * r + 1], self.vp)
        if r >= 2:
            self._go(self.mine(r, 2), self.second.at[3 * r + 2], self.vm, 1)
        if r == 3:
            self._over(self.group(1))
            self._over(self.group(2))

    def far_second(self, r):
        self.post.arrived(self.mine(r, 3), self.second.at[3 * r + 2], self.vm if r < 2 else self.vp)
        self._over(self.mine(r, 3))

    def from_sibling(self):
        self.post.arrived(self.w.at[0:2, :, :, 0:4, :, :, self.cols], self.ends.at[3], self.s.sibling())

    def finish(self):
        self.post.sent(self.w.at[0:3, 0, 0, 0:4, 0, :, self.cols], self.ends.at[0], self.up)
        self.post.sent(self.w.at[0:3, :, 0, 0:4, :, :, self.cols], self.ends.at[1], self.vp)
        self.post.sent(self.w.at[0:2, :, :, 0:4, :, :, self.cols], self.ends.at[2], self.s.sibling())


class Pair:
    def __init__(self, *parts):
        self.parts = parts

    def __getattr__(self, name):
        return lambda *args: [getattr(p, name)(*args) for p in self.parts]


def slot_of(r):
    return (r + 2) % 8


NEAR, FAR = (0, 5), (5, 3)


class RingGather:
    def __init__(self, spot, post, a, sems, count):
        self.s, self.post, self.a, self.sems, self.done = spot, post, a, sems, sems.at[8 * count]
        self.count = count

    def part(self, r, i):
        n = 64 // self.count
        return self.a.at[slot_of(r), pl.ds(n * i, n)]

    def sem(self, way, step, i):
        return self.sems.at[(way * 4 + step) * self.count + i]

    def last(self, way, i):
        return (i < self.count // 2) == (way == 0)

    def own(self, i):
        for way, sign in ((0, 1), (1, -1)):
            self.post.send(self.part(0, i), self.part(-sign, i), self.sem(way, 0, i), self.s.at_z(sign)[1], self.done)

    def step(self, k, i):
        for way, sign in ((0, 1), (1, -1)):
            if k == 4 and not self.last(way, i):
                continue
            ref = self.part(-sign * k, i)
            self.post.arrived(ref, self.sem(way, k - 1, i), self.s.at_z(-sign)[1])
            if k < 3 or (k == 3 and self.last(way, i)):
                self.post.send(ref, self.part(-sign * (k + 1), i), self.sem(way, k, i), self.s.at_z(sign)[1], self.done)

    def finish(self):
        self.post.sent(self.a.at[0:7], self.done, self.s.at_z(1)[1])


def local(src, dst, sem):
    made = pltpu.make_async_copy(src, dst, sem)
    made.start()
    return made


def turn_tables():
    frequency = 10000.0 ** (-(np.arange(DK) // 2 * 2) / DK)
    sign = np.where(np.arange(DK) % 2 == 0, -1.0, 1.0)
    far = (np.arange(8) * 128.0)[:, None] * frequency[None]
    near = np.arange(128.0)[:, None] * frequency[None]
    table_far = np.stack([np.cos(far), np.sin(far)]).astype(np.float32)
    table_near = np.stack([np.cos(near), np.sin(near)]).astype(np.float32)
    return table_far, table_near, sign.astype(np.float32)[None]


def rms(values, gain):
    scale = lax.rsqrt(jnp.mean(values * values, axis=-1, keepdims=True) + 1e-06)
    return (values * scale * gain).astype(BF16)


def silu(v):
    return v / (1.0 + jnp.exp(-v))


def layer_kernel(
    tok_in, q_in, k_in, v_in, g_in, o_in, fg_in, fu_in, gain, mlp_gain, decay, length, far, near, sign,
    res, hid,
    tok, q, k, v, g, o, fg, fu, wa, wb, nrm, small, smallw, tokw, wao, wbb, acts, acts2, kv, cosine, sine, qs, gs, runs, column, gated,
    part, got, out_box, rbuf, box,
    zsem, zr1, zr2, rr, planes1, planes2, planes3, misc, lsem, hsem, isem,
):
    s = Spot()
    post = Post()

    def plane(which, w, cols):
        return Pair(*[
            PlaneGather(s, post, w, cols, way, *[p.at[2 * which + way] for p in (planes1, planes2, planes3)])
            for way in range(2)
        ])

    plane_a = plane(0, wao, pl.ds(0, 1536))
    plane_o = plane(1, wao, pl.ds(1536, 512))
    plane_b = plane(2, wbb, pl.ds(0, CB))
    ring1, ring2 = RingGather(s, post, acts, zr1, 2), RingGather(s, post, acts2, zr2, 4)
    barrier = pltpu.get_barrier_semaphore()
    peers = [s.at_z(n)[1] for n in range(1, 8)] + plane_a.parts[0].neighbours() + [s.partner()]
    for peer in peers:
        pl.semaphore_signal(barrier, inc=1, device_id=peer, device_id_type=MESH)

    brought = ((tok_in, tok), (q_in, q), (k_in, k), (v_in, v), (g_in, g), (o_in, o), (fg_in, fg), (fu_in, fu))
    loads = [local(src, dst, isem.at[n]) for n, (src, dst) in enumerate(brought)]
    for load in loads:
        load.wait()

    for h in range(H):
        wa[h, :, 0:256] = q[:, h * 256 : h * 256 + 256].astype(BF16)
        wa[h, :, 256:512] = k[:, h * 256 : h * 256 + 256].astype(BF16)
        wa[h, :, 512:1024] = v[:, h * 512 : h * 512 + 512].astype(BF16)
        wa[h, :, 1024:1536] = g[:, h * 512 : h * 512 + 512].astype(BF16)
        wa[h, :, 1536:2048] = o[:, h * 512 : h * 512 + 512].astype(BF16)
        wb[h, :, 0:512] = fg[:, h * 512 : h * 512 + 512].astype(BF16)
        wb[h, :, 512:1024] = fu[:, h * 512 : h * 512 + 512].astype(BF16)
    nrm[...] = rms(tok[...].astype(F32), gain[...])
    total = decay[...]
    lane = lax.broadcasted_iota(jnp.int32, (H, SPAN), 1)
    reach = 1
    while reach < SPAN:
        total = total + jnp.where(lane >= reach, pltpu.roll(total, reach, 1), 0.0)
        reach *= 2
    row = lax.broadcasted_iota(jnp.int32, (H, SPAN), 0)
    chosen = jnp.sum(jnp.where(row == s.z, total, 0.0), axis=0, keepdims=True)
    small[...] = jnp.where(row < 4, chosen, length[0, 0])

    pl.semaphore_wait(barrier, len(peers))

    def trade(src, dst, which):
        return pltpu.make_async_remote_copy(
            src_ref=src, dst_ref=dst, send_sem=lsem.at[which], recv_sem=misc.at[which],
            device_id=s.partner(), device_id_type=MESH,
        )

    own_a = local(wa.at[s.z], wao.at[s.y, s.xh, s.c, s.z, s.xl], lsem.at[0])
    own_b = local(wb.at[s.z], wbb.at[s.y, s.xh, s.c, s.z, s.xl], lsem.at[3])

    @pl.when(jnp.logical_not(s.same))
    def _():
        trade(nrm, acts.at[slot_of(0)], 1).start()
        trade(tok, tokw, 2).start()

    @pl.when(s.same)
    def _():
        local(nrm, acts.at[slot_of(0)], lsem.at[1])
        local(tok, tokw, lsem.at[2])

    early, late = pl.ds(0, 1536), pl.ds(1536, 512)
    for cols, sem in ((early, 0), (late, 4)):
        for n in (4, 3, 5, 2, 6, 1, 7):
            zd, peer = s.at_z(n)
            dst = wao.at[s.y, s.xh, s.c, s.z, s.xl, :, cols]
            post.send(wa.at[zd, :, cols], dst, zsem.at[sem], peer, zsem.at[sem + 1])
    post.send(small, smallw, misc.at[0], s.sibling(), misc.at[6])

    base = pl.multiple_of(64 * s.c, 64)
    cn, sn = near[0, pl.ds(base, 64)], near[1, pl.ds(base, 64)]
    for i in range(8):
        b, _ = s.at_z(i - 2)
        cf, sf = far[0, pl.ds(b, 1)], far[1, pl.ds(b, 1)]
        cosine[i] = cf * cn - sf * sn
        sine[i] = (sf * cn + cf * sn) * sign[...]

    @pl.when(s.same)
    def _():
        pltpu.make_async_copy(nrm, acts.at[slot_of(0)], lsem.at[1]).wait()

    @pl.when(jnp.logical_not(s.same))
    def _():
        trade(nrm, acts.at[slot_of(0)], 1).wait_recv()

    own_a.wait()
    post.arrived(wao.at[s.y, s.xh, s.c, 0:7, s.xl, :, early], zsem.at[0], s.at_z(1)[1])

    plane_a.own()
    ring1.own(0)
    ring1.own(1)

    post.arrived(smallw, misc.at[0], s.sibling())
    runs[...] = jnp.where(s.same, small[...], smallw[...])
    pieces = [runs[0:1, pl.ds(pl.multiple_of(128 * s.at_z(i - 2)[0], 128), 128)] for i in range(8)]
    run_row = jnp.concatenate(pieces, axis=1)
    column[...] = jnp.broadcast_to(run_row, (128, SPAN)).T
    last = runs[4:5, 0:1]
    at = lax.rem(lax.broadcasted_iota(jnp.int32, (1, SPAN), 1) + 128 * (s.z + 6), SPAN)

    plane_a.near_first()
    post.arrived(wao.at[s.y, s.xh, s.c, 0:7, s.xl, :, late], zsem.at[4], s.at_z(1)[1])
    plane_o.own()
    ring1.step(1, 0)
    ring1.step(1, 1)
    plane_a.far_first()
    plane_a.near_second(0)
    ring1.step(2, 0)
    plane_a.near_second(1)
    ring1.step(2, 1)
    plane_a.near_second(2)
    plane_a.near_second(3)
    plane_o.near_first()
    ring1.step(3, 0)
    plane_a.far_second(0)
    plane_a.far_second(1)
    ring1.step(3, 1)
    plane_a.far_second(2)
    plane_a.far_second(3)
    plane_o.far_first()
    plane_a.from_sibling()

    weights_a = wao.reshape(D, CA)
    weights_b = wbb.reshape(D, CB)

    def project(span, low, width):
        first, count = span
        rows = acts[first : first + count].reshape(64 * count, D)
        return jnp.dot(rows, weights_a[:, low : low + width], preferred_element_type=F32)

    def rot(u, span):
        first, count = span
        n = 64 * count
        even = lax.rem(lax.broadcasted_iota(jnp.int32, (n, DK), 1), 2) == 0
        swapped = jnp.where(even, pltpu.roll(u, DK - 1, 1), pltpu.roll(u, 1, 1))
        turned = u * cosine[first : first + count].reshape(n, DK) + swapped * sine[first : first + count].reshape(n, DK)
        return turned.astype(BF16)

    def key_part(span):
        first, count = span
        kv[first : first + count, s.c, :, 0:256] = rot(project(span, 256, 256), span).reshape(count, 64, 256)

    def value_part(span, which):
        first, count = span
        made = project(span, 512 + 256 * which, 256).astype(BF16).reshape(count, 64, 256)
        kv[first : first + count, s.c, :, 256 + 256 * which : 512 + 256 * which] = made

    def query_part(span):
        first, count = span
        qs[64 * first : 64 * (first + count)] = rot(project(span, 0, 256), span)

    def gate_part(span, which):
        first, count = span
        made = project(span, 1024 + 256 * which, 256).astype(BF16)
        gs[64 * first : 64 * (first + count), 256 * which : 256 * which + 256] = made

    def share(span, arrive):
        mine = kv.at[pl.ds(*span), s.c]
        post.send(mine, mine, misc.at[arrive], s.sibling(), misc.at[7])

    def shared(span, arrive):
        post.arrived(kv.at[pl.ds(*span), 1 - s.c], misc.at[arrive], s.sibling())

    def retain(span):
        first, count = span
        n = 64 * count
        rows = slice(64 * first, 64 * (first + count))
        keys = kv[:, :, :, 0:256].reshape(SPAN, 256)
        values = kv[:, :, :, 256:768].reshape(SPAN, 512)
        scores = lax.dot_general(qs[rows], keys, (((1,), (1,)), ((), ())), preferred_element_type=F32) * (DK**-0.5)
        step = lax.broadcasted_iota(jnp.int32, (n, 1), 0)
        block = lax.div(step, 64)
        place = 128 * lax.rem(block + (s.z + first + 6), 8) + 64 * s.c + (step - 64 * block)
        run_col = jnp.concatenate(
            [column[pl.ds(pl.multiple_of(128 * i + 64 * s.c, 64), 64), 0:1] for i in range(first, first + count)], axis=0
        )
        weights = (scores * jnp.exp(jnp.where(place >= at, run_col - run_row, -jnp.inf))).astype(BF16)
        kept = jnp.dot(weights, values, preferred_element_type=F32)
        mean = jnp.mean(kept, axis=-1, keepdims=True)
        spread = jnp.mean(kept * kept, axis=-1, keepdims=True) - mean * mean
        normed = (kept - mean) * lax.rsqrt(spread + 1e-05)
        live = place.astype(F32) < last
        gated[rows] = jnp.where(live, silu(gs[rows].astype(F32)) * normed, 0.0).astype(BF16)

    def put_out(span):
        first, count = span
        rows = slice(64 * first, 64 * (first + count))
        for tile in range(4):
            wo = weights_a[512 * tile : 512 * tile + 512, 1536:2048]
            made = lax.dot_general(gated[rows], wo, (((1,), (1,)), ((), ())), preferred_element_type=F32)
            part[first : first + count, :, 512 * tile : 512 * tile + 512] = made.astype(BF16).reshape(count, 64, 512)

    key_part(NEAR)
    value_part(NEAR, 0)
    plane_o.near_second(0)
    plane_o.near_second(1)
    value_part(NEAR, 1)
    share(NEAR, 3)
    ring1.step(4, 0)
    ring1.step(4, 1)
    plane_o.near_second(2)
    plane_o.near_second(3)
    for n in (4, 3, 5, 2, 6, 1, 7):
        zd, peer = s.at_z(n)
        post.send(wb.at[zd], wbb.at[s.y, s.xh, s.c, s.z, s.xl], zsem.at[2], peer, zsem.at[3])
    key_part(FAR)
    value_part(FAR, 0)
    value_part(FAR, 1)
    share(FAR, 4)
    query_part(FAR)
    gate_part(FAR, 0)
    gate_part(FAR, 1)
    plane_o.far_second(0)
    plane_o.far_second(1)
    plane_o.far_second(2)
    plane_o.far_second(3)
    shared(NEAR, 3)
    shared(FAR, 4)
    retain(FAR)
    plane_o.from_sibling()
    put_out(FAR)

    ways = ((0, 1), (1, -1))

    def rows(i):
        return pl.ds(16 * i, 16)

    def rs_send(way, hop, i, src):
        arrive = rr.at[(way * 4 + hop) * 4 + i]
        post.send(src, got.at[way, hop, rows(i)], arrive, s.at_z(ways[way][1])[1], rr.at[32])

    def rs_wait(way, hop, i):
        post.arrived(got.at[way, hop, rows(i)], rr.at[(way * 4 + hop) * 4 + i], s.at_z(-ways[way][1])[1])

    def relay(hop, way, i):
        rs_wait(way, hop - 1, i)
        here = part[slot_of((4 - hop) * ways[way][1]), rows(i)].astype(F32)
        both = here + got[way, hop - 1, rows(i)].astype(F32)
        out_box[way, hop - 1, rows(i)] = both.astype(BF16)
        rs_send(way, hop, i, out_box.at[way, hop - 1, rows(i)])

    def relay_both(hop, i):
        for way in range(2):
            relay(hop, way, i)

    for way, sign in ways:
        for i in (2 * way, 2 * way + 1):
            rs_send(way, 0, i, part.at[slot_of(4), rows(i)])
        for i in (2 - 2 * way, 3 - 2 * way):
            rs_send(way, 1, i, part.at[slot_of(3 * sign), rows(i)])
    own_b.wait()
    post.arrived(wbb.at[s.y, s.xh, s.c, 0:7, s.xl], zsem.at[2], s.at_z(1)[1])
    plane_b.own()
    query_part(NEAR)
    gate_part(NEAR, 0)
    gate_part(NEAR, 1)
    for way, i in ((0, 0), (1, 2), (0, 1), (1, 3)):
        relay(1, way, i)
    retain(NEAR)
    plane_b.near_first()
    put_out(NEAR)
    for i in (2, 0, 3, 1):
        relay_both(2, i)
    plane_b.far_first()
    plane_b.near_second(0)
    for i in (2, 0, 3, 1):
        relay_both(3, i)
    plane_b.near_second(1)
    plane_b.near_second(2)
    plane_b.far_second(0)

    for half in (2, 0, 3, 1):
        for way in range(2):
            rs_wait(way, 3, half)
        branch = (
            part[slot_of(0), rows(half)].astype(F32)
            + got[0, 3, rows(half)].astype(F32)
            + got[1, 3, rows(half)].astype(F32)
        )
        residual = (tokw_ready(s, trade, tok, tokw, lsem, half)[rows(half)].astype(F32) + branch).astype(BF16)
        rbuf[rows(half)] = residual
        acts2[slot_of(0), rows(half)] = rms(residual.astype(F32), mlp_gain[...])
        ring2.own(half)

    def hand_back():
        return pltpu.make_async_remote_copy(
            src_ref=rbuf, dst_ref=res, send_sem=lsem.at[4], recv_sem=misc.at[5],
            device_id=s.partner(), device_id_type=MESH,
        )

    @pl.when(s.same)
    def _():
        local(rbuf, res, lsem.at[4])

    @pl.when(jnp.logical_not(s.same))
    def _():
        hand_back().start()

    def hide(span, j, slot):
        first, count = span
        low = pl.multiple_of(256 * j, 256)
        high = pl.multiple_of(256 * j + 512, 256)
        rows2 = acts2[first : first + count].reshape(64 * count, D)
        gate = jnp.dot(rows2, weights_b[:, pl.ds(low, 256)], preferred_element_type=F32)
        up = jnp.dot(rows2, weights_b[:, pl.ds(high, 256)], preferred_element_type=F32)
        box[slot, first : first + count] = (silu(gate) * up).astype(BF16).reshape(count, 64, 256)

    def give(slot, i, peer, arrive):
        b, _ = s.at_z(i - 2)
        return pltpu.make_async_remote_copy(
            src_ref=box.at[slot, i], dst_ref=hid.at[b, s.c], send_sem=hsem.at[slot], recv_sem=hsem.at[arrive],
            device_id=peer, device_id_type=MESH,
        )

    def keep(i):
        b, _ = s.at_z(i - 2)
        return pltpu.make_async_copy(box.at[1, i], hid.at[b, s.c], hsem.at[1])

    def give_far(span):
        first, count = span

        @pl.when(s.same)
        def _():
            for i in range(first, first + count):
                give(0, i, s.across(), 2).start()

        @pl.when(jnp.logical_not(s.same))
        def _():
            for i in range(first, first + count):
                give(0, i, s.partner(), 3).start()

    def give_near(span):
        first, count = span

        @pl.when(s.same)
        def _():
            for i in range(first, first + count):
                keep(i).start()

        @pl.when(jnp.logical_not(s.same))
        def _():
            for i in range(first, first + count):
                give(1, i, s.sibling(), 4).start()

    plane_b.near_second(3)
    plane_b.far_second(1)
    plane_b.far_second(2)
    for i in (2, 0, 3, 1):
        ring2.step(1, i)
    plane_b.far_second(3)
    for i in (2, 0, 3, 1):
        ring2.step(2, i)
    plane_b.from_sibling()
    hide(NEAR, 1 - s.xl, 0)
    give_far(NEAR)
    for i in (2, 0, 3, 1):
        ring2.step(3, i)
    hide(NEAR, s.xl, 1)
    give_near(NEAR)
    for i in (2, 0, 3, 1):
        ring2.step(4, i)
    hide(FAR, 1 - s.xl, 0)
    give_far(FAR)
    hide(FAR, s.xl, 1)
    give_near(FAR)

    @pl.when(s.same)
    def _():
        pltpu.make_async_copy(rbuf, res, lsem.at[4]).wait()
        pltpu.make_async_copy(box.at[1], hid.at[:, s.c], hsem.at[1]).wait()
        post.sent(box.at[0], hsem.at[0], s.across())
        post.arrived(hid.at[:, 1 - s.c], hsem.at[4], s.sibling())

    @pl.when(jnp.logical_not(s.same))
    def _():
        hand_back().wait()
        trade(nrm, acts.at[slot_of(0)], 1).wait_send()
        trade(tok, tokw, 2).wait_send()
        post.sent(box.at[0], hsem.at[0], s.partner())
        post.sent(box.at[1], hsem.at[1], s.sibling())
        post.arrived(hid.at[:, s.c], hsem.at[2], s.across())
        post.arrived(hid.at[:, 1 - s.c], hsem.at[3], s.partner())

    post.sent(wa.at[0:7, :, early], zsem.at[1], s.at_z(1)[1])
    post.sent(wa.at[0:7, :, late], zsem.at[5], s.at_z(1)[1])
    post.sent(wb.at[0:7], zsem.at[3], s.at_z(1)[1])
    post.sent(small, misc.at[6], s.sibling())
    post.sent(kv.at[:, s.c], misc.at[7], s.sibling())
    post.sent(part.at[0:7], rr.at[32], s.at_z(1)[1])
    for each in (plane_a, plane_o, plane_b, ring1, ring2):
        each.finish()


def tokw_ready(s, trade, tok, tokw, lsem, half):
    if half == 2:

        @pl.when(s.same)
        def _():
            pltpu.make_async_copy(tok, tokw, lsem.at[2]).wait()

        @pl.when(jnp.logical_not(s.same))
        def _():
            trade(tok, tokw, 2).wait_recv()

    return tokw


def layer(*args):
    dma = lambda *n: pltpu.SemaphoreType.DMA(n)
    return pl.pallas_call(
        layer_kernel,
        out_shape=(jax.ShapeDtypeStruct((ROWS, D), BF16), jax.ShapeDtypeStruct((8, 2, ROWS, 256), BF16)),
        in_specs=[ANY] * 8 + [VM] * 3 + [SM] + [VM] * 3,
        out_specs=(ANY, ANY),
        scratch_shapes=[
            pltpu.VMEM((ROWS, D), BF16),
            *[pltpu.VMEM((8, n), F32) for n in (2048, 2048, 4096, 4096, 4096, 4096, 4096)],
            pltpu.VMEM((8, 8, CA), BF16),
            pltpu.VMEM((8, 8, CB), BF16),
            pltpu.VMEM((ROWS, D), BF16),
            pltpu.VMEM((8, SPAN), F32),
            pltpu.VMEM((8, SPAN), F32),
            pltpu.VMEM((ROWS, D), BF16),
            pltpu.VMEM((4, 2, 2, 8, 2, 8, CA), BF16),
            pltpu.VMEM((4, 2, 2, 8, 2, 8, CB), BF16),
            pltpu.VMEM((8, ROWS, D), BF16),
            pltpu.VMEM((8, ROWS, D), BF16),
            pltpu.VMEM((8, 2, ROWS, 768), BF16),
            pltpu.VMEM((8, ROWS, DK), F32),
            pltpu.VMEM((8, ROWS, DK), F32),
            pltpu.VMEM((512, DK), BF16),
            pltpu.VMEM((512, DV), BF16),
            pltpu.VMEM((8, SPAN), F32),
            pltpu.VMEM((SPAN, 128), F32),
            pltpu.VMEM((512, DV), BF16),
            pltpu.VMEM((8, ROWS, D), BF16),
            pltpu.VMEM((2, 4, ROWS, D), BF16),
            pltpu.VMEM((2, 3, ROWS, D), BF16),
            pltpu.VMEM((ROWS, D), BF16),
            pltpu.VMEM((2, 8, ROWS, 256), BF16),
            dma(6), dma(17), dma(33), dma(33),
            dma(6, PlaneGather.FIRST), dma(6, PlaneGather.SECOND), dma(6, PlaneGather.ENDS),
            dma(8), dma(5), dma(5), dma(8),
        ],
        compiler_params=pltpu.CompilerParams(collective_id=0, has_side_effects=True, vmem_limit_bytes=VMEM_LIMIT),
        name="layer",
    )(*args)


def finish_kernel(res, hid, res_out, hid_out):
    res_out[...] = res[...]
    hid_out[...] = hid[...]


def finish(res, hid):
    return pl.pallas_call(
        finish_kernel,
        out_shape=(jax.ShapeDtypeStruct(res.shape, BF16), jax.ShapeDtypeStruct(hid.shape, BF16)),
        in_specs=[VM] * 2,
        out_specs=(VM, VM),
        name="finish",
    )(res, hid)


def per_device(tokens, norm_gain, mlp_gain, lengths, log_decay, q, k, v, g, o, fg, fu):
    far, near, sign = turn_tables()
    res, hid = layer(
        tokens, q, k, v, g, o.T, fg, fu,
        norm_gain.reshape(1, D), mlp_gain.reshape(1, D), log_decay.T, lengths.astype(F32).reshape(1, 1), far, near, sign,
    )
    return finish(res, hid.reshape(SPAN, 256))


def solution(mesh):
    rows = P(("dp", "mp"), None)
    placed = (rows, P(), P(), P("dp"), P("dp", None), rows, rows, rows, rows, P(None, ("dp", "mp")), rows, rows)
    return jax.shard_map(
        per_device, mesh=mesh, in_specs=placed, out_specs=(rows, P("dp", "mp")), check_vma=False
    )
```

```python
import functools
import math

import jax
import jax.numpy as jnp
import numpy as np
from jax import lax
from jax.experimental import pallas as pl
from jax.experimental.pallas import tpu as pltpu
from jax.sharding import PartitionSpec as P

MESH = pl.DeviceIdType.MESH
F32, BF16 = jnp.float32, jnp.bfloat16
D, H, DK, DV = 2048, 8, 256, 512
SPAN, ROWS = 1024, 64
CA, CB = 2048, 1024
VMEM_LIMIT = 64 * 1024 * 1024 - 65536
ANY = pl.BlockSpec(memory_space=pl.ANY)
SM = pl.BlockSpec(memory_space=pltpu.SMEM)
VM = pl.BlockSpec(memory_space=pltpu.VMEM)


class Spot:
    def __init__(self):
        dp, mp = lax.axis_index("dp"), lax.axis_index("mp")
        self.dp, self.mp = dp, mp
        self.y = lax.div(dp, 4)
        self.c = lax.rem(dp, 2)
        self.z = lax.div(mp, 2)
        self.xl = lax.rem(mp, 2)
        self.xh = lax.rem(lax.div(dp, 2), 2)
        self.x = self.xh * 2 + self.xl
        self.same = self.c == self.xl

    def at_z(self, step):
        z = lax.rem(self.z + (step + 8), 8)
        return z, (self.dp, z * 2 + self.xl)

    def sibling(self):
        return (self.dp + 1 - 2 * self.c, self.mp)

    def partner(self):
        return (self.dp + 1 - 2 * self.c, self.mp + 1 - 2 * self.xl)

    def across(self):
        return (self.dp, self.mp + 1 - 2 * self.xl)

    def plane(self, x, y):
        return (y * 4 + lax.div(x, 2) * 2 + self.c, self.z * 2 + lax.rem(x, 2))


class Post:
    def copy(self, src, dst, arrive, peer, done):
        return pltpu.make_async_remote_copy(
            src_ref=src, dst_ref=dst, send_sem=done, recv_sem=arrive, device_id=peer, device_id_type=MESH
        )

    def send(self, src, dst, arrive, peer, done):
        self.copy(src, dst, arrive, peer, done).start()

    def arrived(self, ref, arrive, peer):
        self.copy(ref, ref, arrive, peer, arrive).wait_recv()

    def sent(self, ref, done, peer):
        self.copy(ref, ref, done, peer, done).wait_send()


class PlaneGather:
    FIRST, SECOND, ENDS = 4, 12, 4

    def __init__(self, spot, post, w, cols, way, first, second, ends):
        self.s, self.post, self.w, self.cols, self.way = spot, post, w, cols, way
        self.first, self.second, self.ends = first, second, ends
        u, v = (spot.y, spot.x) if way else (spot.x, spot.y)
        ring = lambda a, k: lax.rem(a + (k + 4), 4)
        order = (0, -1, 1, 2)
        self.us, self.vs = [ring(u, k) for k in order], [ring(v, k) for k in order]
        self.up, self.um = self.peer(ring(u, 1), v), self.peer(ring(u, -1), v)
        self.vp, self.vm = self.peer(u, ring(v, 1)), self.peer(u, ring(v, -1))

    def xy(self, u, v):
        return (v, u) if self.way else (u, v)

    def peer(self, u, v):
        return self.s.plane(*self.xy(u, v))

    def rows(self, half):
        return pl.ds(4 * self.way, 4) if half is None else pl.ds(4 * self.way + 2 * half, 2)

    def mine(self, r, t, half=None):
        x, y = self.xy(self.us[r], self.vs[t])
        return self.w.at[y, lax.div(x, 2), self.s.c, self.rows(half), lax.rem(x, 2), :, self.cols]

    def group(self, t):
        v, c, rows = self.vs[t], self.s.c, self.rows(None)
        if self.way:
            return self.w.at[:, lax.div(v, 2), c, rows, lax.rem(v, 2), :, self.cols]
        return self.w.at[v, :, c, rows, :, :, self.cols]

    def neighbours(self):
        return [self.up, self.um, self.vp, self.vm, self.s.sibling()]

    def _go(self, ref, arrive, peer, end):
        self.post.send(ref, ref, arrive, peer, self.ends.at[end])

    def _over(self, ref):
        self._go(ref, self.ends.at[3], self.s.sibling(), 2)

    def own_first(self):
        ref = self.mine(0, 0)
        self._go(ref, self.first.at[0], self.up, 0)
        self._go(ref, self.first.at[1], self.um, 0)

    def own_row(self):
        self._row(0)

    def _row(self, r):
        ref = self.mine(r, 0)
        self._go(ref, self.second.at[3 * r], self.vp, 1)
        self._go(ref, self.second.at[3 * r + 1], self.vm, 1)

    def near_first(self):
        self.post.arrived(self.mine(1, 0), self.first.at[0], self.um)
        self._go(self.mine(1, 0, 0), self.first.at[2], self.up, 0)
        self.post.arrived(self.mine(2, 0), self.first.at[1], self.up)
        self._go(self.mine(2, 0, 1), self.first.at[3], self.um, 0)

    def near_rows(self):
        self._row(1)
        self._row(2)

    def far_first(self):
        self.post.arrived(self.mine(3, 0, 0), self.first.at[2], self.um)
        self.post.arrived(self.mine(3, 0, 1), self.first.at[3], self.up)
        self._row(3)
        self._over(self.group(0))

    def near_second(self, r):
        self.post.arrived(self.mine(r, 1), self.second.at[3 * r], self.vm)
        if r < 2:
            self._go(self.mine(r, 1), self.second.at[3 * r + 2], self.vp, 1)
        self.post.arrived(self.mine(r, 2), self.second.at[3 * r + 1], self.vp)
        if r >= 2:
            self._go(self.mine(r, 2), self.second.at[3 * r + 2], self.vm, 1)
        if r == 3:
            self._over(self.group(1))
            self._over(self.group(2))

    def far_second(self, r):
        self.post.arrived(self.mine(r, 3), self.second.at[3 * r + 2], self.vm if r < 2 else self.vp)
        self._over(self.mine(r, 3))

    def from_sibling(self):
        self.post.arrived(self.w.at[0:2, :, :, 0:4, :, :, self.cols], self.ends.at[3], self.s.sibling())

    def finish(self):
        self.post.sent(self.w.at[0:3, 0, 0, 0:4, 0, :, self.cols], self.ends.at[0], self.up)
        self.post.sent(self.w.at[0:3, :, 0, 0:4, :, :, self.cols], self.ends.at[1], self.vp)
        self.post.sent(self.w.at[0:2, :, :, 0:4, :, :, self.cols], self.ends.at[2], self.s.sibling())


class Pair:
    def __init__(self, *parts):
        self.parts = parts

    def __getattr__(self, name):
        return lambda *args: [getattr(p, name)(*args) for p in self.parts]


def slot_of(r):
    return (r + 2) % 8


NEAR, FAR = (0, 5), (5, 3)


class RingGather:
    def __init__(self, spot, post, a, sems, count):
        self.s, self.post, self.a, self.sems, self.done = spot, post, a, sems, sems.at[8 * count]
        self.count = count

    def part(self, r, i):
        n = 64 // self.count
        return self.a.at[slot_of(r), pl.ds(n * i, n)]

    def sem(self, way, step, i):
        return self.sems.at[(way * 4 + step) * self.count + i]

    def last(self, way, i):
        return (i < self.count // 2) == (way == 0)

    def own(self, i):
        for way, sign in ((0, 1), (1, -1)):
            self.post.send(self.part(0, i), self.part(-sign, i), self.sem(way, 0, i), self.s.at_z(sign)[1], self.done)

    def step(self, k, i):
        for way, sign in ((0, 1), (1, -1)):
            if k == 4 and not self.last(way, i):
                continue
            ref = self.part(-sign * k, i)
            self.post.arrived(ref, self.sem(way, k - 1, i), self.s.at_z(-sign)[1])
            if k < 3 or (k == 3 and self.last(way, i)):
                self.post.send(ref, self.part(-sign * (k + 1), i), self.sem(way, k, i), self.s.at_z(sign)[1], self.done)

    def finish(self):
        self.post.sent(self.a.at[0:7], self.done, self.s.at_z(1)[1])


def local(src, dst, sem):
    made = pltpu.make_async_copy(src, dst, sem)
    made.start()
    return made


def turn_tables():
    frequency = 10000.0 ** (-(np.arange(DK) // 2 * 2) / DK)
    sign = np.where(np.arange(DK) % 2 == 0, -1.0, 1.0)
    far = (np.arange(8) * 128.0)[:, None] * frequency[None]
    near = np.arange(128.0)[:, None] * frequency[None]
    table_far = np.stack([np.cos(far), np.sin(far)]).astype(np.float32)
    table_near = np.stack([np.cos(near), np.sin(near)]).astype(np.float32)
    return table_far, table_near, sign.astype(np.float32)[None]


def rms(values, gain):
    scale = lax.rsqrt(jnp.mean(values * values, axis=-1, keepdims=True) + 1e-06)
    return (values * scale * gain).astype(BF16)


def silu(v):
    return v / (1.0 + jnp.exp(-v))


def layer_kernel(
    tok_in, q_in, k_in, v_in, g_in, o_in, fg_in, fu_in, gain, mlp_gain, decay, length, far, near, sign,
    res, hid,
    tok, q, k, v, g, o, fg, fu, wa, wb, nrm, small, smallw, tokw, wao, wbb, acts, acts2, kv, cosine, sine, qs, gs, runs, column, gated,
    part, got, out_box, rbuf, box,
    zsem, zr1, zr2, rr, planes1, planes2, planes3, misc, lsem, hsem, isem,
):
    s = Spot()
    post = Post()

    def plane(which, w, cols):
        return Pair(*[
            PlaneGather(s, post, w, cols, way, *[p.at[2 * which + way] for p in (planes1, planes2, planes3)])
            for way in range(2)
        ])

    plane_a = plane(0, wao, pl.ds(0, 1536))
    plane_o = plane(1, wao, pl.ds(1536, 512))
    plane_b = plane(2, wbb, pl.ds(0, CB))
    ring1, ring2 = RingGather(s, post, acts, zr1, 2), RingGather(s, post, acts2, zr2, 4)
    barrier = pltpu.get_barrier_semaphore()
    peers = [s.at_z(n)[1] for n in range(1, 8)] + plane_a.parts[0].neighbours() + [s.partner()]
    for peer in peers:
        pl.semaphore_signal(barrier, inc=1, device_id=peer, device_id_type=MESH)

    brought = ((tok_in, tok), (q_in, q), (k_in, k), (v_in, v), (g_in, g), (o_in, o), (fg_in, fg), (fu_in, fu))
    loads = [local(src, dst, isem.at[n]) for n, (src, dst) in enumerate(brought)]
    for load in loads:
        load.wait()

    for h in range(H):
        wa[h, :, 0:256] = q[:, h * 256 : h * 256 + 256].astype(BF16)
        wa[h, :, 256:512] = k[:, h * 256 : h * 256 + 256].astype(BF16)
        wa[h, :, 512:1024] = v[:, h * 512 : h * 512 + 512].astype(BF16)
        wa[h, :, 1024:1536] = g[:, h * 512 : h * 512 + 512].astype(BF16)
        wa[h, :, 1536:2048] = o[:, h * 512 : h * 512 + 512].astype(BF16)
        wb[h, :, 0:512] = fg[:, h * 512 : h * 512 + 512].astype(BF16)
        wb[h, :, 512:1024] = fu[:, h * 512 : h * 512 + 512].astype(BF16)
    nrm[...] = rms(tok[...].astype(F32), gain[...])
    total = decay[...]
    lane = lax.broadcasted_iota(jnp.int32, (H, SPAN), 1)
    reach = 1
    while reach < SPAN:
        total = total + jnp.where(lane >= reach, pltpu.roll(total, reach, 1), 0.0)
        reach *= 2
    row = lax.broadcasted_iota(jnp.int32, (H, SPAN), 0)
    chosen = jnp.sum(jnp.where(row == s.z, total, 0.0), axis=0, keepdims=True)
    small[...] = jnp.where(row < 4, chosen, length[0, 0])

    pl.semaphore_wait(barrier, len(peers))

    def trade(src, dst, which):
        return pltpu.make_async_remote_copy(
            src_ref=src, dst_ref=dst, send_sem=lsem.at[which], recv_sem=misc.at[which],
            device_id=s.partner(), device_id_type=MESH,
        )

    own_a = local(wa.at[s.z], wao.at[s.y, s.xh, s.c, s.z, s.xl], lsem.at[0])
    own_b = local(wb.at[s.z], wbb.at[s.y, s.xh, s.c, s.z, s.xl], lsem.at[3])

    @pl.when(jnp.logical_not(s.same))
    def _():
        trade(nrm, acts.at[slot_of(0)], 1).start()
        trade(tok, tokw, 2).start()

    @pl.when(s.same)
    def _():
        local(nrm, acts.at[slot_of(0)], lsem.at[1])
        local(tok, tokw, lsem.at[2])

    early, late = pl.ds(0, 1536), pl.ds(1536, 512)
    for cols, sem in ((early, 0), (late, 4)):
        for n in (4, 3, 5, 2, 6, 1, 7):
            zd, peer = s.at_z(n)
            dst = wao.at[s.y, s.xh, s.c, s.z, s.xl, :, cols]
            post.send(wa.at[zd, :, cols], dst, zsem.at[sem], peer, zsem.at[sem + 1])
    post.send(small, smallw, misc.at[0], s.sibling(), misc.at[6])

    base = pl.multiple_of(64 * s.c, 64)
    cn, sn = near[0, pl.ds(base, 64)], near[1, pl.ds(base, 64)]
    for i in range(8):
        b, _ = s.at_z(i - 2)
        cf, sf = far[0, pl.ds(b, 1)], far[1, pl.ds(b, 1)]
        cosine[i] = cf * cn - sf * sn
        sine[i] = (sf * cn + cf * sn) * sign[...]

    @pl.when(s.same)
    def _():
        pltpu.make_async_copy(nrm, acts.at[slot_of(0)], lsem.at[1]).wait()

    @pl.when(jnp.logical_not(s.same))
    def _():
        trade(nrm, acts.at[slot_of(0)], 1).wait_recv()

    own_a.wait()
    post.arrived(wao.at[s.y, s.xh, s.c, 0:7, s.xl, :, early], zsem.at[0], s.at_z(1)[1])

    plane_a.own_first()
    plane_a.own_row()
    ring1.own(0)
    ring1.own(1)

    post.arrived(smallw, misc.at[0], s.sibling())
    runs[...] = jnp.where(s.same, small[...], smallw[...])
    pieces = [runs[0:1, pl.ds(pl.multiple_of(128 * s.at_z(i - 2)[0], 128), 128)] for i in range(8)]
    run_row = jnp.concatenate(pieces, axis=1)
    column[...] = jnp.broadcast_to(run_row, (128, SPAN)).T
    last = runs[4:5, 0:1]
    at = lax.rem(lax.broadcasted_iota(jnp.int32, (1, SPAN), 1) + 128 * (s.z + 6), SPAN)

    post.arrived(wao.at[s.y, s.xh, s.c, 0:7, s.xl, :, late], zsem.at[4], s.at_z(1)[1])
    plane_o.own_first()
    plane_a.near_first()
    plane_a.near_rows()
    ring1.step(1, 0)
    ring1.step(1, 1)
    plane_a.far_first()
    plane_o.near_first()
    plane_o.own_row()
    plane_a.near_second(0)
    ring1.step(2, 0)
    plane_a.near_second(1)
    ring1.step(2, 1)
    plane_a.near_second(2)
    plane_a.near_second(3)
    plane_o.near_rows()
    ring1.step(3, 0)
    plane_a.far_second(0)
    plane_a.far_second(1)
    ring1.step(3, 1)
    plane_a.far_second(2)
    plane_a.far_second(3)
    plane_o.far_first()
    plane_a.from_sibling()

    weights_a = wao.reshape(D, CA)
    weights_b = wbb.reshape(D, CB)

    def project(span, low, width):
        first, count = span
        rows = acts[first : first + count].reshape(64 * count, D)
        return jnp.dot(rows, weights_a[:, low : low + width], preferred_element_type=F32)

    def rot(u, span):
        first, count = span
        n = 64 * count
        even = lax.rem(lax.broadcasted_iota(jnp.int32, (n, DK), 1), 2) == 0
        swapped = jnp.where(even, pltpu.roll(u, DK - 1, 1), pltpu.roll(u, 1, 1))
        turned = u * cosine[first : first + count].reshape(n, DK) + swapped * sine[first : first + count].reshape(n, DK)
        return turned.astype(BF16)

    def key_part(span):
        first, count = span
        kv[first : first + count, s.c, :, 0:256] = rot(project(span, 256, 256), span).reshape(count, 64, 256)

    def value_part(span, which):
        first, count = span
        made = project(span, 512 + 256 * which, 256).astype(BF16).reshape(count, 64, 256)
        kv[first : first + count, s.c, :, 256 + 256 * which : 512 + 256 * which] = made

    def query_part(span):
        first, count = span
        qs[64 * first : 64 * (first + count)] = rot(project(span, 0, 256), span)

    def gate_part(span, which):
        first, count = span
        made = project(span, 1024 + 256 * which, 256).astype(BF16)
        gs[64 * first : 64 * (first + count), 256 * which : 256 * which + 256] = made

    def share(span, arrive):
        mine = kv.at[pl.ds(*span), s.c]
        post.send(mine, mine, misc.at[arrive], s.sibling(), misc.at[7])

    def shared(span, arrive):
        post.arrived(kv.at[pl.ds(*span), 1 - s.c], misc.at[arrive], s.sibling())

    def retain(span):
        first, count = span
        n = 64 * count
        rows = slice(64 * first, 64 * (first + count))
        keys = kv[:, :, :, 0:256].reshape(SPAN, 256)
        values = kv[:, :, :, 256:768].reshape(SPAN, 512)
        scores = lax.dot_general(qs[rows], keys, (((1,), (1,)), ((), ())), preferred_element_type=F32) * (DK**-0.5)
        step = lax.broadcasted_iota(jnp.int32, (n, 1), 0)
        block = lax.div(step, 64)
        place = 128 * lax.rem(block + (s.z + first + 6), 8) + 64 * s.c + (step - 64 * block)
        run_col = jnp.concatenate(
            [column[pl.ds(pl.multiple_of(128 * i + 64 * s.c, 64), 64), 0:1] for i in range(first, first + count)], axis=0
        )
        weights = (scores * jnp.exp(jnp.where(place >= at, run_col - run_row, -jnp.inf))).astype(BF16)
        kept = jnp.dot(weights, values, preferred_element_type=F32)
        mean = jnp.mean(kept, axis=-1, keepdims=True)
        spread = jnp.mean(kept * kept, axis=-1, keepdims=True) - mean * mean
        normed = (kept - mean) * lax.rsqrt(spread + 1e-05)
        live = place.astype(F32) < last
        gated[rows] = jnp.where(live, silu(gs[rows].astype(F32)) * normed, 0.0).astype(BF16)

    def put_out(span):
        first, count = span
        rows = slice(64 * first, 64 * (first + count))
        for tile in range(4):
            wo = weights_a[512 * tile : 512 * tile + 512, 1536:2048]
            made = lax.dot_general(gated[rows], wo, (((1,), (1,)), ((), ())), preferred_element_type=F32)
            part[first : first + count, :, 512 * tile : 512 * tile + 512] = made.astype(BF16).reshape(count, 64, 512)

    key_part(NEAR)
    value_part(NEAR, 0)
    plane_o.near_second(0)
    plane_o.near_second(1)
    value_part(NEAR, 1)
    share(NEAR, 3)
    ring1.step(4, 0)
    ring1.step(4, 1)
    plane_o.near_second(2)
    plane_o.near_second(3)
    for n in (4, 3, 5, 2, 6, 1, 7):
        zd, peer = s.at_z(n)
        post.send(wb.at[zd], wbb.at[s.y, s.xh, s.c, s.z, s.xl], zsem.at[2], peer, zsem.at[3])
    key_part(FAR)
    value_part(FAR, 0)
    value_part(FAR, 1)
    share(FAR, 4)
    query_part(FAR)
    gate_part(FAR, 0)
    gate_part(FAR, 1)
    plane_o.far_second(0)
    plane_o.far_second(1)
    plane_o.far_second(2)
    plane_o.far_second(3)
    shared(NEAR, 3)
    shared(FAR, 4)
    retain(FAR)
    plane_o.from_sibling()
    put_out(FAR)

    ways = ((0, 1), (1, -1))

    def rows(i):
        return pl.ds(16 * i, 16)

    def rs_send(way, hop, i, src):
        arrive = rr.at[(way * 4 + hop) * 4 + i]
        post.send(src, got.at[way, hop, rows(i)], arrive, s.at_z(ways[way][1])[1], rr.at[32])

    def rs_wait(way, hop, i):
        post.arrived(got.at[way, hop, rows(i)], rr.at[(way * 4 + hop) * 4 + i], s.at_z(-ways[way][1])[1])

    def relay(hop, way, i):
        rs_wait(way, hop - 1, i)
        here = part[slot_of((4 - hop) * ways[way][1]), rows(i)].astype(F32)
        both = here + got[way, hop - 1, rows(i)].astype(F32)
        out_box[way, hop - 1, rows(i)] = both.astype(BF16)
        rs_send(way, hop, i, out_box.at[way, hop - 1, rows(i)])

    def relay_both(hop, i):
        for way in range(2):
            relay(hop, way, i)

    for way, sign in ways:
        for i in (2 * way, 2 * way + 1):
            rs_send(way, 0, i, part.at[slot_of(4), rows(i)])
        for i in (2 - 2 * way, 3 - 2 * way):
            rs_send(way, 1, i, part.at[slot_of(3 * sign), rows(i)])
    own_b.wait()
    post.arrived(wbb.at[s.y, s.xh, s.c, 0:7, s.xl], zsem.at[2], s.at_z(1)[1])
    plane_b.own_first()
    plane_b.own_row()
    query_part(NEAR)
    gate_part(NEAR, 0)
    gate_part(NEAR, 1)
    for way, i in ((0, 0), (1, 2), (0, 1), (1, 3)):
        relay(1, way, i)
    retain(NEAR)
    plane_b.near_first()
    plane_b.near_rows()
    put_out(NEAR)
    for i in (2, 0, 3, 1):
        relay_both(2, i)
    plane_b.far_first()
    plane_b.near_second(0)
    for i in (2, 0, 3, 1):
        relay_both(3, i)
    plane_b.near_second(1)
    plane_b.near_second(2)
    plane_b.far_second(0)

    for half in (2, 0, 3, 1):
        for way in range(2):
            rs_wait(way, 3, half)
        branch = (
            part[slot_of(0), rows(half)].astype(F32)
            + got[0, 3, rows(half)].astype(F32)
            + got[1, 3, rows(half)].astype(F32)
        )
        residual = (tokw_ready(s, trade, tok, tokw, lsem, half)[rows(half)].astype(F32) + branch).astype(BF16)
        rbuf[rows(half)] = residual
        acts2[slot_of(0), rows(half)] = rms(residual.astype(F32), mlp_gain[...])
        ring2.own(half)

    def hand_back():
        return pltpu.make_async_remote_copy(
            src_ref=rbuf, dst_ref=res, send_sem=lsem.at[4], recv_sem=misc.at[5],
            device_id=s.partner(), device_id_type=MESH,
        )

    @pl.when(s.same)
    def _():
        local(rbuf, res, lsem.at[4])

    @pl.when(jnp.logical_not(s.same))
    def _():
        hand_back().start()

    def hide(slots, j, slot):
        low = pl.multiple_of(256 * j, 256)
        high = pl.multiple_of(256 * j + 512, 256)
        rows2 = jnp.concatenate([acts2[i] for i in slots], axis=0)
        gate = jnp.dot(rows2, weights_b[:, pl.ds(low, 256)], preferred_element_type=F32)
        up = jnp.dot(rows2, weights_b[:, pl.ds(high, 256)], preferred_element_type=F32)
        made = (silu(gate) * up).astype(BF16)
        for n, i in enumerate(slots):
            box[slot, i] = made[64 * n : 64 * n + 64]

    def give(slot, i, peer, arrive):
        b, _ = s.at_z(i - 2)
        return pltpu.make_async_remote_copy(
            src_ref=box.at[slot, i], dst_ref=hid.at[b, s.c], send_sem=hsem.at[slot], recv_sem=hsem.at[arrive],
            device_id=peer, device_id_type=MESH,
        )

    def keep(i):
        b, _ = s.at_z(i - 2)
        return pltpu.make_async_copy(box.at[1, i], hid.at[b, s.c], hsem.at[1])

    def give_far(slots):
        @pl.when(s.same)
        def _():
            for i in slots:
                give(0, i, s.across(), 2).start()

        @pl.when(jnp.logical_not(s.same))
        def _():
            for i in slots:
                give(0, i, s.partner(), 3).start()

    def give_near(slots):
        @pl.when(s.same)
        def _():
            for i in slots:
                keep(i).start()

        @pl.when(jnp.logical_not(s.same))
        def _():
            for i in slots:
                give(1, i, s.sibling(), 4).start()

    plane_b.near_second(3)
    plane_b.far_second(1)
    plane_b.far_second(2)
    for i in (2, 0, 3, 1):
        ring2.step(1, i)
    plane_b.far_second(3)
    for i in (2, 0, 3, 1):
        ring2.step(2, i)
    plane_b.from_sibling()
    hide(range(0, 5), 1 - s.xl, 0)
    give_far(range(0, 5))
    for i in (2, 0, 3, 1):
        ring2.step(3, i)
    hide((5, 7), 1 - s.xl, 0)
    give_far((5, 7))
    hide(range(0, 5), s.xl, 1)
    give_near(range(0, 5))
    for i in (2, 0, 3, 1):
        ring2.step(4, i)
    hide((6,), 1 - s.xl, 0)
    give_far((6,))
    hide((5, 6, 7), s.xl, 1)
    give_near((5, 6, 7))

    @pl.when(s.same)
    def _():
        pltpu.make_async_copy(rbuf, res, lsem.at[4]).wait()
        pltpu.make_async_copy(box.at[1], hid.at[:, s.c], hsem.at[1]).wait()
        post.sent(box.at[0], hsem.at[0], s.across())
        post.arrived(hid.at[:, 1 - s.c], hsem.at[4], s.sibling())

    @pl.when(jnp.logical_not(s.same))
    def _():
        hand_back().wait()
        trade(nrm, acts.at[slot_of(0)], 1).wait_send()
        trade(tok, tokw, 2).wait_send()
        post.sent(box.at[0], hsem.at[0], s.partner())
        post.sent(box.at[1], hsem.at[1], s.sibling())
        post.arrived(hid.at[:, s.c], hsem.at[2], s.across())
        post.arrived(hid.at[:, 1 - s.c], hsem.at[3], s.partner())

    post.sent(wa.at[0:7, :, early], zsem.at[1], s.at_z(1)[1])
    post.sent(wa.at[0:7, :, late], zsem.at[5], s.at_z(1)[1])
    post.sent(wb.at[0:7], zsem.at[3], s.at_z(1)[1])
    post.sent(small, misc.at[6], s.sibling())
    post.sent(kv.at[:, s.c], misc.at[7], s.sibling())
    post.sent(part.at[0:7], rr.at[32], s.at_z(1)[1])
    for each in (plane_a, plane_o, plane_b, ring1, ring2):
        each.finish()


def tokw_ready(s, trade, tok, tokw, lsem, half):
    if half == 2:

        @pl.when(s.same)
        def _():
            pltpu.make_async_copy(tok, tokw, lsem.at[2]).wait()

        @pl.when(jnp.logical_not(s.same))
        def _():
            trade(tok, tokw, 2).wait_recv()

    return tokw


def layer(*args):
    dma = lambda *n: pltpu.SemaphoreType.DMA(n)
    return pl.pallas_call(
        layer_kernel,
        out_shape=(jax.ShapeDtypeStruct((ROWS, D), BF16), jax.ShapeDtypeStruct((8, 2, ROWS, 256), BF16)),
        in_specs=[ANY] * 8 + [VM] * 3 + [SM] + [VM] * 3,
        out_specs=(ANY, ANY),
        scratch_shapes=[
            pltpu.VMEM((ROWS, D), BF16),
            *[pltpu.VMEM((8, n), F32) for n in (2048, 2048, 4096, 4096, 4096, 4096, 4096)],
            pltpu.VMEM((8, 8, CA), BF16),
            pltpu.VMEM((8, 8, CB), BF16),
            pltpu.VMEM((ROWS, D), BF16),
            pltpu.VMEM((8, SPAN), F32),
            pltpu.VMEM((8, SPAN), F32),
            pltpu.VMEM((ROWS, D), BF16),
            pltpu.VMEM((4, 2, 2, 8, 2, 8, CA), BF16),
            pltpu.VMEM((4, 2, 2, 8, 2, 8, CB), BF16),
            pltpu.VMEM((8, ROWS, D), BF16),
            pltpu.VMEM((8, ROWS, D), BF16),
            pltpu.VMEM((8, 2, ROWS, 768), BF16),
            pltpu.VMEM((8, ROWS, DK), F32),
            pltpu.VMEM((8, ROWS, DK), F32),
            pltpu.VMEM((512, DK), BF16),
            pltpu.VMEM((512, DV), BF16),
            pltpu.VMEM((8, SPAN), F32),
            pltpu.VMEM((SPAN, 128), F32),
            pltpu.VMEM((512, DV), BF16),
            pltpu.VMEM((8, ROWS, D), BF16),
            pltpu.VMEM((2, 4, ROWS, D), BF16),
            pltpu.VMEM((2, 3, ROWS, D), BF16),
            pltpu.VMEM((ROWS, D), BF16),
            pltpu.VMEM((2, 8, ROWS, 256), BF16),
            dma(6), dma(17), dma(33), dma(33),
            dma(6, PlaneGather.FIRST), dma(6, PlaneGather.SECOND), dma(6, PlaneGather.ENDS),
            dma(8), dma(5), dma(5), dma(8),
        ],
        compiler_params=pltpu.CompilerParams(collective_id=0, has_side_effects=True, vmem_limit_bytes=VMEM_LIMIT),
        name="layer",
    )(*args)


def finish_kernel(res, hid, res_out, hid_out):
    res_out[...] = res[...]
    hid_out[...] = hid[...]


def finish(res, hid):
    return pl.pallas_call(
        finish_kernel,
        out_shape=(jax.ShapeDtypeStruct(res.shape, BF16), jax.ShapeDtypeStruct(hid.shape, BF16)),
        in_specs=[VM] * 2,
        out_specs=(VM, VM),
        name="finish",
    )(res, hid)


def per_device(tokens, norm_gain, mlp_gain, lengths, log_decay, q, k, v, g, o, fg, fu):
    far, near, sign = turn_tables()
    res, hid = layer(
        tokens, q, k, v, g, o.T, fg, fu,
        norm_gain.reshape(1, D), mlp_gain.reshape(1, D), log_decay.T, lengths.astype(F32).reshape(1, 1), far, near, sign,
    )
    return finish(res, hid.reshape(SPAN, 256))


def solution(mesh):
    rows = P(("dp", "mp"), None)
    placed = (rows, P(), P(), P("dp"), P("dp", None), rows, rows, rows, rows, P(None, ("dp", "mp")), rows, rows)
    return jax.shard_map(
        per_device, mesh=mesh, in_specs=placed, out_specs=(rows, P("dp", "mp")), check_vma=False
    )
```

```python
import functools
import math

import jax
import jax.numpy as jnp
import numpy as np
from jax import lax
from jax.experimental import pallas as pl
from jax.experimental.pallas import tpu as pltpu
from jax.sharding import PartitionSpec as P

MESH = pl.DeviceIdType.MESH
F32, BF16 = jnp.float32, jnp.bfloat16
D, H, DK, DV = 2048, 8, 256, 512
SPAN, ROWS = 1024, 64
CA, CB = 2048, 1024
VMEM_LIMIT = 64 * 1024 * 1024 - 65536
ANY = pl.BlockSpec(memory_space=pl.ANY)
SM = pl.BlockSpec(memory_space=pltpu.SMEM)
VM = pl.BlockSpec(memory_space=pltpu.VMEM)


class Spot:
    def __init__(self):
        dp, mp = lax.axis_index("dp"), lax.axis_index("mp")
        self.dp, self.mp = dp, mp
        self.y = lax.div(dp, 4)
        self.c = lax.rem(dp, 2)
        self.z = lax.div(mp, 2)
        self.xl = lax.rem(mp, 2)
        self.xh = lax.rem(lax.div(dp, 2), 2)
        self.x = self.xh * 2 + self.xl
        self.same = self.c == self.xl

    def at_z(self, step):
        z = lax.rem(self.z + (step + 8), 8)
        return z, (self.dp, z * 2 + self.xl)

    def sibling(self):
        return (self.dp + 1 - 2 * self.c, self.mp)

    def partner(self):
        return (self.dp + 1 - 2 * self.c, self.mp + 1 - 2 * self.xl)

    def across(self):
        return (self.dp, self.mp + 1 - 2 * self.xl)

    def plane(self, x, y):
        return (y * 4 + lax.div(x, 2) * 2 + self.c, self.z * 2 + lax.rem(x, 2))


class Post:
    def copy(self, src, dst, arrive, peer, done):
        return pltpu.make_async_remote_copy(
            src_ref=src, dst_ref=dst, send_sem=done, recv_sem=arrive, device_id=peer, device_id_type=MESH
        )

    def send(self, src, dst, arrive, peer, done):
        self.copy(src, dst, arrive, peer, done).start()

    def arrived(self, ref, arrive, peer):
        self.copy(ref, ref, arrive, peer, arrive).wait_recv()

    def sent(self, ref, done, peer):
        self.copy(ref, ref, done, peer, done).wait_send()


class PlaneGather:
    FIRST, SECOND, ENDS = 4, 12, 4

    def __init__(self, spot, post, w, cols, way, first, second, ends):
        self.s, self.post, self.w, self.cols, self.way = spot, post, w, cols, way
        self.first, self.second, self.ends = first, second, ends
        u, v = (spot.y, spot.x) if way else (spot.x, spot.y)
        ring = lambda a, k: lax.rem(a + (k + 4), 4)
        order = (0, -1, 1, 2)
        self.us, self.vs = [ring(u, k) for k in order], [ring(v, k) for k in order]
        self.up, self.um = self.peer(ring(u, 1), v), self.peer(ring(u, -1), v)
        self.vp, self.vm = self.peer(u, ring(v, 1)), self.peer(u, ring(v, -1))

    def xy(self, u, v):
        return (v, u) if self.way else (u, v)

    def peer(self, u, v):
        return self.s.plane(*self.xy(u, v))

    def rows(self, half):
        return pl.ds(4 * self.way, 4) if half is None else pl.ds(4 * self.way + 2 * half, 2)

    def mine(self, r, t, half=None):
        x, y = self.xy(self.us[r], self.vs[t])
        return self.w.at[y, lax.div(x, 2), self.s.c, self.rows(half), lax.rem(x, 2), :, self.cols]

    def group(self, t):
        v, c, rows = self.vs[t], self.s.c, self.rows(None)
        if self.way:
            return self.w.at[:, lax.div(v, 2), c, rows, lax.rem(v, 2), :, self.cols]
        return self.w.at[v, :, c, rows, :, :, self.cols]

    def neighbours(self):
        return [self.up, self.um, self.vp, self.vm, self.s.sibling()]

    def _go(self, ref, arrive, peer, end):
        self.post.send(ref, ref, arrive, peer, self.ends.at[end])

    def _over(self, ref):
        self._go(ref, self.ends.at[3], self.s.sibling(), 2)

    def own_first(self):
        ref = self.mine(0, 0)
        self._go(ref, self.first.at[0], self.up, 0)
        self._go(ref, self.first.at[1], self.um, 0)

    def own_row(self):
        self._row(0)

    def _row(self, r):
        ref = self.mine(r, 0)
        self._go(ref, self.second.at[3 * r], self.vp, 1)
        self._go(ref, self.second.at[3 * r + 1], self.vm, 1)

    def near_first(self):
        self.post.arrived(self.mine(1, 0), self.first.at[0], self.um)
        self._go(self.mine(1, 0, 0), self.first.at[2], self.up, 0)
        self.post.arrived(self.mine(2, 0), self.first.at[1], self.up)
        self._go(self.mine(2, 0, 1), self.first.at[3], self.um, 0)

    def near_rows(self):
        self._row(1)
        self._row(2)

    def far_first(self):
        self.post.arrived(self.mine(3, 0, 0), self.first.at[2], self.um)
        self.post.arrived(self.mine(3, 0, 1), self.first.at[3], self.up)
        self._row(3)
        self._over(self.group(0))

    def near_second(self, r):
        self.post.arrived(self.mine(r, 1), self.second.at[3 * r], self.vm)
        if r < 2:
            self._go(self.mine(r, 1), self.second.at[3 * r + 2], self.vp, 1)
        self.post.arrived(self.mine(r, 2), self.second.at[3 * r + 1], self.vp)
        if r >= 2:
            self._go(self.mine(r, 2), self.second.at[3 * r + 2], self.vm, 1)
        if r == 3:
            self._over(self.group(1))
            self._over(self.group(2))

    def far_second(self, r):
        self.post.arrived(self.mine(r, 3), self.second.at[3 * r + 2], self.vm if r < 2 else self.vp)
        self._over(self.mine(r, 3))

    def from_sibling(self):
        self.post.arrived(self.w.at[0:2, :, :, 0:4, :, :, self.cols], self.ends.at[3], self.s.sibling())

    def finish(self):
        self.post.sent(self.w.at[0:3, 0, 0, 0:4, 0, :, self.cols], self.ends.at[0], self.up)
        self.post.sent(self.w.at[0:3, :, 0, 0:4, :, :, self.cols], self.ends.at[1], self.vp)
        self.post.sent(self.w.at[0:2, :, :, 0:4, :, :, self.cols], self.ends.at[2], self.s.sibling())


class Pair:
    def __init__(self, *parts):
        self.parts = parts

    def __getattr__(self, name):
        return lambda *args: [getattr(p, name)(*args) for p in self.parts]


def slot_of(r):
    return (r + 2) % 8


NEAR, FAR = (0, 5), (5, 3)


class RingGather:
    def __init__(self, spot, post, a, sems, count):
        self.s, self.post, self.a, self.sems, self.done = spot, post, a, sems, sems.at[8 * count]
        self.count = count

    def part(self, r, i):
        n = 64 // self.count
        return self.a.at[slot_of(r), pl.ds(n * i, n)]

    def sem(self, way, step, i):
        return self.sems.at[(way * 4 + step) * self.count + i]

    def last(self, way, i):
        return (i < self.count // 2) == (way == 0)

    def own(self, i):
        for way, sign in ((0, 1), (1, -1)):
            self.post.send(self.part(0, i), self.part(-sign, i), self.sem(way, 0, i), self.s.at_z(sign)[1], self.done)

    def step(self, k, i):
        for way, sign in ((0, 1), (1, -1)):
            if k == 4 and not self.last(way, i):
                continue
            ref = self.part(-sign * k, i)
            self.post.arrived(ref, self.sem(way, k - 1, i), self.s.at_z(-sign)[1])
            if k < 3 or (k == 3 and self.last(way, i)):
                self.post.send(ref, self.part(-sign * (k + 1), i), self.sem(way, k, i), self.s.at_z(sign)[1], self.done)

    def finish(self):
        self.post.sent(self.a.at[0:7], self.done, self.s.at_z(1)[1])


def local(src, dst, sem):
    made = pltpu.make_async_copy(src, dst, sem)
    made.start()
    return made


def turn_tables():
    frequency = 10000.0 ** (-(np.arange(DK) // 2 * 2) / DK)
    sign = np.where(np.arange(DK) % 2 == 0, -1.0, 1.0)
    far = (np.arange(8) * 128.0)[:, None] * frequency[None]
    near = np.arange(128.0)[:, None] * frequency[None]
    table_far = np.stack([np.cos(far), np.sin(far)]).astype(np.float32)
    table_near = np.stack([np.cos(near), np.sin(near)]).astype(np.float32)
    return table_far, table_near, sign.astype(np.float32)[None]


def rms(values, gain):
    scale = lax.rsqrt(jnp.mean(values * values, axis=-1, keepdims=True) + 1e-06)
    return (values * scale * gain).astype(BF16)


def silu(v):
    return v / (1.0 + jnp.exp(-v))


def layer_kernel(
    tok_in, q_in, k_in, v_in, g_in, o_in, fg_in, fu_in, gain, mlp_gain, decay, length, far, near, sign,
    res, hid,
    tok, q, k, v, g, o, fg, fu, wa, wb, nrm, small, smallw, tokw, wao, wbb, acts, acts2, kv, cosine, sine, qs, gs, runs, column, gated,
    part, got, out_box, rbuf, box,
    zsem, zr1, zr2, rr, planes1, planes2, planes3, misc, lsem, hsem, isem,
):
    s = Spot()
    post = Post()

    def plane(which, w, cols):
        return Pair(*[
            PlaneGather(s, post, w, cols, way, *[p.at[2 * which + way] for p in (planes1, planes2, planes3)])
            for way in range(2)
        ])

    plane_a = plane(0, wao, pl.ds(0, 1536))
    plane_o = plane(1, wao, pl.ds(1536, 512))
    plane_b = plane(2, wbb, pl.ds(0, CB))
    ring1, ring2 = RingGather(s, post, acts, zr1, 2), RingGather(s, post, acts2, zr2, 4)
    barrier = pltpu.get_barrier_semaphore()
    peers = [s.at_z(n)[1] for n in range(1, 8)] + plane_a.parts[0].neighbours() + [s.partner()]
    for peer in peers:
        pl.semaphore_signal(barrier, inc=1, device_id=peer, device_id_type=MESH)

    brought = ((tok_in, tok), (q_in, q), (k_in, k), (v_in, v), (g_in, g), (o_in, o), (fg_in, fg), (fu_in, fu))
    loads = [local(src, dst, isem.at[n]) for n, (src, dst) in enumerate(brought)]
    for load in loads:
        load.wait()

    for h in range(H):
        wa[h, :, 0:256] = q[:, h * 256 : h * 256 + 256].astype(BF16)
        wa[h, :, 256:512] = k[:, h * 256 : h * 256 + 256].astype(BF16)
        wa[h, :, 512:1024] = v[:, h * 512 : h * 512 + 512].astype(BF16)
        wa[h, :, 1024:1536] = g[:, h * 512 : h * 512 + 512].astype(BF16)
        wa[h, :, 1536:2048] = o[:, h * 512 : h * 512 + 512].astype(BF16)
        wb[h, :, 0:512] = fg[:, h * 512 : h * 512 + 512].astype(BF16)
        wb[h, :, 512:1024] = fu[:, h * 512 : h * 512 + 512].astype(BF16)
    nrm[...] = rms(tok[...].astype(F32), gain[...])
    total = decay[...]
    lane = lax.broadcasted_iota(jnp.int32, (H, SPAN), 1)
    reach = 1
    while reach < SPAN:
        total = total + jnp.where(lane >= reach, pltpu.roll(total, reach, 1), 0.0)
        reach *= 2
    row = lax.broadcasted_iota(jnp.int32, (H, SPAN), 0)
    chosen = jnp.sum(jnp.where(row == s.z, total, 0.0), axis=0, keepdims=True)
    small[...] = jnp.where(row < 4, chosen, length[0, 0])

    pl.semaphore_wait(barrier, len(peers))

    def trade(src, dst, which):
        return pltpu.make_async_remote_copy(
            src_ref=src, dst_ref=dst, send_sem=lsem.at[which], recv_sem=misc.at[which],
            device_id=s.partner(), device_id_type=MESH,
        )

    own_a = local(wa.at[s.z], wao.at[s.y, s.xh, s.c, s.z, s.xl], lsem.at[0])
    own_b = local(wb.at[s.z], wbb.at[s.y, s.xh, s.c, s.z, s.xl], lsem.at[3])

    @pl.when(jnp.logical_not(s.same))
    def _():
        trade(nrm, acts.at[slot_of(0)], 1).start()
        trade(tok, tokw, 2).start()

    @pl.when(s.same)
    def _():
        local(nrm, acts.at[slot_of(0)], lsem.at[1])
        local(tok, tokw, lsem.at[2])

    early, late = pl.ds(0, 1536), pl.ds(1536, 512)
    for cols, sem in ((early, 0), (late, 4)):
        for n in (4, 3, 5, 2, 6, 1, 7):
            zd, peer = s.at_z(n)
            dst = wao.at[s.y, s.xh, s.c, s.z, s.xl, :, cols]
            post.send(wa.at[zd, :, cols], dst, zsem.at[sem], peer, zsem.at[sem + 1])
    post.send(small, smallw, misc.at[0], s.sibling(), misc.at[6])

    base = pl.multiple_of(64 * s.c, 64)
    cn, sn = near[0, pl.ds(base, 64)], near[1, pl.ds(base, 64)]
    for i in range(8):
        b, _ = s.at_z(i - 2)
        cf, sf = far[0, pl.ds(b, 1)], far[1, pl.ds(b, 1)]
        cosine[i] = cf * cn - sf * sn
        sine[i] = (sf * cn + cf * sn) * sign[...]

    @pl.when(s.same)
    def _():
        pltpu.make_async_copy(nrm, acts.at[slot_of(0)], lsem.at[1]).wait()

    @pl.when(jnp.logical_not(s.same))
    def _():
        trade(nrm, acts.at[slot_of(0)], 1).wait_recv()

    own_a.wait()
    post.arrived(wao.at[s.y, s.xh, s.c, 0:7, s.xl, :, early], zsem.at[0], s.at_z(1)[1])

    plane_a.own_first()
    plane_a.own_row()
    ring1.own(0)
    ring1.own(1)

    post.arrived(smallw, misc.at[0], s.sibling())
    runs[...] = jnp.where(s.same, small[...], smallw[...])
    pieces = [runs[0:1, pl.ds(pl.multiple_of(128 * s.at_z(i - 2)[0], 128), 128)] for i in range(8)]
    run_row = jnp.concatenate(pieces, axis=1)
    column[...] = jnp.broadcast_to(run_row, (128, SPAN)).T
    last = runs[4:5, 0:1]
    at = lax.rem(lax.broadcasted_iota(jnp.int32, (1, SPAN), 1) + 128 * (s.z + 6), SPAN)

    post.arrived(wao.at[s.y, s.xh, s.c, 0:7, s.xl, :, late], zsem.at[4], s.at_z(1)[1])
    plane_o.own_first()
    plane_a.near_first()
    plane_a.near_rows()
    ring1.step(1, 0)
    ring1.step(1, 1)
    plane_a.far_first()
    plane_o.near_first()
    plane_o.own_row()
    plane_a.near_second(0)
    ring1.step(2, 0)
    plane_a.near_second(1)
    ring1.step(2, 1)
    plane_a.near_second(2)
    plane_a.near_second(3)
    plane_o.near_rows()
    ring1.step(3, 0)
    plane_a.far_second(0)
    plane_a.far_second(1)
    ring1.step(3, 1)
    plane_a.far_second(2)
    plane_a.far_second(3)
    plane_o.far_first()
    plane_a.from_sibling()

    weights_a = wao.reshape(D, CA)
    weights_b = wbb.reshape(D, CB)

    def project(span, low, width):
        first, count = span
        rows = acts[first : first + count].reshape(64 * count, D)
        return jnp.dot(rows, weights_a[:, low : low + width], preferred_element_type=F32)

    def rot(u, span):
        first, count = span
        n = 64 * count
        even = lax.rem(lax.broadcasted_iota(jnp.int32, (n, DK), 1), 2) == 0
        swapped = jnp.where(even, pltpu.roll(u, DK - 1, 1), pltpu.roll(u, 1, 1))
        turned = u * cosine[first : first + count].reshape(n, DK) + swapped * sine[first : first + count].reshape(n, DK)
        return turned.astype(BF16)

    def key_part(span):
        first, count = span
        kv[first : first + count, s.c, :, 0:256] = rot(project(span, 256, 256), span).reshape(count, 64, 256)

    def value_part(span, which):
        first, count = span
        made = project(span, 512 + 256 * which, 256).astype(BF16).reshape(count, 64, 256)
        kv[first : first + count, s.c, :, 256 + 256 * which : 512 + 256 * which] = made

    def query_part(span):
        first, count = span
        qs[64 * first : 64 * (first + count)] = rot(project(span, 0, 256), span)

    def gate_part(span, which):
        first, count = span
        made = project(span, 1024 + 256 * which, 256).astype(BF16)
        gs[64 * first : 64 * (first + count), 256 * which : 256 * which + 256] = made

    def share(span, arrive):
        mine = kv.at[pl.ds(*span), s.c]
        post.send(mine, mine, misc.at[arrive], s.sibling(), misc.at[7])

    def shared(span, arrive):
        post.arrived(kv.at[pl.ds(*span), 1 - s.c], misc.at[arrive], s.sibling())

    def retain(span):
        first, count = span
        n = 64 * count
        rows = slice(64 * first, 64 * (first + count))
        keys = kv[:, :, :, 0:256].reshape(SPAN, 256)
        values = kv[:, :, :, 256:768].reshape(SPAN, 512)
        scores = lax.dot_general(qs[rows], keys, (((1,), (1,)), ((), ())), preferred_element_type=F32) * (DK**-0.5)
        step = lax.broadcasted_iota(jnp.int32, (n, 1), 0)
        block = lax.div(step, 64)
        place = 128 * lax.rem(block + (s.z + first + 6), 8) + 64 * s.c + (step - 64 * block)
        run_col = jnp.concatenate(
            [column[pl.ds(pl.multiple_of(128 * i + 64 * s.c, 64), 64), 0:1] for i in range(first, first + count)], axis=0
        )
        weights = (scores * jnp.exp(jnp.where(place >= at, run_col - run_row, -jnp.inf))).astype(BF16)
        kept = jnp.dot(weights, values, preferred_element_type=F32)
        mean = jnp.mean(kept, axis=-1, keepdims=True)
        spread = jnp.mean(kept * kept, axis=-1, keepdims=True) - mean * mean
        normed = (kept - mean) * lax.rsqrt(spread + 1e-05)
        live = place.astype(F32) < last
        gated[rows] = jnp.where(live, silu(gs[rows].astype(F32)) * normed, 0.0).astype(BF16)

    def put_out(span):
        first, count = span
        rows = slice(64 * first, 64 * (first + count))
        for tile in range(4):
            wo = weights_a[512 * tile : 512 * tile + 512, 1536:2048]
            made = lax.dot_general(gated[rows], wo, (((1,), (1,)), ((), ())), preferred_element_type=F32)
            part[first : first + count, :, 512 * tile : 512 * tile + 512] = made.astype(BF16).reshape(count, 64, 512)

    key_part(NEAR)
    value_part(NEAR, 0)
    plane_o.near_second(0)
    plane_o.near_second(1)
    value_part(NEAR, 1)
    share(NEAR, 3)
    ring1.step(4, 0)
    ring1.step(4, 1)
    plane_o.near_second(2)
    plane_o.near_second(3)
    for n in (4, 3, 5, 2, 6, 1, 7):
        zd, peer = s.at_z(n)
        post.send(wb.at[zd], wbb.at[s.y, s.xh, s.c, s.z, s.xl], zsem.at[2], peer, zsem.at[3])
    key_part(FAR)
    value_part(FAR, 0)
    value_part(FAR, 1)
    share(FAR, 4)
    query_part(FAR)
    gate_part(FAR, 0)
    gate_part(FAR, 1)
    plane_o.far_second(0)
    plane_o.far_second(1)
    plane_o.far_second(2)
    plane_o.far_second(3)
    shared(NEAR, 3)
    shared(FAR, 4)
    retain(FAR)
    plane_o.from_sibling()
    put_out(FAR)

    ways = ((0, 1), (1, -1))

    def rows(i):
        return pl.ds(16 * i, 16)

    def rs_send(way, hop, i, src):
        arrive = rr.at[(way * 4 + hop) * 4 + i]
        post.send(src, got.at[way, hop, rows(i)], arrive, s.at_z(ways[way][1])[1], rr.at[32])

    def rs_wait(way, hop, i):
        post.arrived(got.at[way, hop, rows(i)], rr.at[(way * 4 + hop) * 4 + i], s.at_z(-ways[way][1])[1])

    def relay(hop, way, i):
        rs_wait(way, hop - 1, i)
        here = part[slot_of((4 - hop) * ways[way][1]), rows(i)].astype(F32)
        both = here + got[way, hop - 1, rows(i)].astype(F32)
        out_box[way, hop - 1, rows(i)] = both.astype(BF16)
        rs_send(way, hop, i, out_box.at[way, hop - 1, rows(i)])

    def relay_both(hop, i):
        for way in range(2):
            relay(hop, way, i)

    for way, sign in ways:
        for i in (2 * way, 2 * way + 1):
            rs_send(way, 0, i, part.at[slot_of(4), rows(i)])
        for i in (2 - 2 * way, 3 - 2 * way):
            rs_send(way, 1, i, part.at[slot_of(3 * sign), rows(i)])
    own_b.wait()
    post.arrived(wbb.at[s.y, s.xh, s.c, 0:7, s.xl], zsem.at[2], s.at_z(1)[1])
    plane_b.own_first()
    plane_b.own_row()
    query_part(NEAR)
    gate_part(NEAR, 0)
    gate_part(NEAR, 1)
    for way, i in ((0, 0), (1, 2), (0, 1), (1, 3)):
        relay(1, way, i)
    retain(NEAR)
    plane_b.near_first()
    plane_b.near_rows()
    put_out(NEAR)
    for i in (2, 0, 3, 1):
        relay_both(2, i)
    plane_b.far_first()
    plane_b.near_second(0)
    for i in (2, 0, 3, 1):
        relay_both(3, i)
    plane_b.near_second(1)
    plane_b.near_second(2)
    plane_b.far_second(0)

    for half in (2, 0, 3, 1):
        for way in range(2):
            rs_wait(way, 3, half)
        branch = (
            part[slot_of(0), rows(half)].astype(F32)
            + got[0, 3, rows(half)].astype(F32)
            + got[1, 3, rows(half)].astype(F32)
        )
        residual = (tokw_ready(s, trade, tok, tokw, lsem, half)[rows(half)].astype(F32) + branch).astype(BF16)
        rbuf[rows(half)] = residual
        acts2[slot_of(0), rows(half)] = rms(residual.astype(F32), mlp_gain[...])
        ring2.own(half)

    def hand_back():
        return pltpu.make_async_remote_copy(
            src_ref=rbuf, dst_ref=res, send_sem=lsem.at[4], recv_sem=misc.at[5],
            device_id=s.partner(), device_id_type=MESH,
        )

    @pl.when(s.same)
    def _():
        local(rbuf, res, lsem.at[4])

    @pl.when(jnp.logical_not(s.same))
    def _():
        hand_back().start()

    def hide(slots, j, slot):
        low = pl.multiple_of(256 * j, 256)
        high = pl.multiple_of(256 * j + 512, 256)
        rows2 = jnp.concatenate([acts2[i] for i in slots], axis=0)
        gate = jnp.dot(rows2, weights_b[:, pl.ds(low, 256)], preferred_element_type=F32)
        up = jnp.dot(rows2, weights_b[:, pl.ds(high, 256)], preferred_element_type=F32)
        made = (silu(gate) * up).astype(BF16)
        for n, i in enumerate(slots):
            box[slot, i] = made[64 * n : 64 * n + 64]

    def give(slot, i, peer, arrive):
        b, _ = s.at_z(i - 2)
        return pltpu.make_async_remote_copy(
            src_ref=box.at[slot, i], dst_ref=hid.at[b, s.c], send_sem=hsem.at[slot], recv_sem=hsem.at[arrive],
            device_id=peer, device_id_type=MESH,
        )

    def keep(i):
        b, _ = s.at_z(i - 2)
        return pltpu.make_async_copy(box.at[1, i], hid.at[b, s.c], hsem.at[1])

    def give_far(slots):
        @pl.when(s.same)
        def _():
            for i in slots:
                give(0, i, s.across(), 2).start()

        @pl.when(jnp.logical_not(s.same))
        def _():
            for i in slots:
                give(0, i, s.partner(), 3).start()

    def give_near(slots):
        @pl.when(s.same)
        def _():
            for i in slots:
                keep(i).start()

        @pl.when(jnp.logical_not(s.same))
        def _():
            for i in slots:
                give(1, i, s.sibling(), 4).start()

    plane_b.near_second(3)
    plane_b.far_second(1)
    plane_b.far_second(2)
    for i in (2, 0, 3, 1):
        ring2.step(1, i)
    plane_b.far_second(3)
    for i in (2, 0, 3, 1):
        ring2.step(2, i)
    plane_b.from_sibling()
    hide(range(0, 5), 1 - s.xl, 0)
    give_far(range(0, 5))
    for i in (2, 0, 3, 1):
        ring2.step(3, i)
    hide((5, 7), 1 - s.xl, 0)
    give_far((5, 7))
    hide(range(0, 5), s.xl, 1)
    give_near(range(0, 5))
    for i in (2, 0, 3, 1):
        ring2.step(4, i)
    hide((6,), 1 - s.xl, 0)
    give_far((6,))
    hide((5, 6, 7), s.xl, 1)
    give_near((5, 6, 7))

    @pl.when(s.same)
    def _():
        pltpu.make_async_copy(rbuf, res, lsem.at[4]).wait()
        pltpu.make_async_copy(box.at[1], hid.at[:, s.c], hsem.at[1]).wait()
        post.sent(box.at[0], hsem.at[0], s.across())
        post.arrived(hid.at[:, 1 - s.c], hsem.at[4], s.sibling())

    @pl.when(jnp.logical_not(s.same))
    def _():
        hand_back().wait()
        trade(nrm, acts.at[slot_of(0)], 1).wait_send()
        trade(tok, tokw, 2).wait_send()
        post.sent(box.at[0], hsem.at[0], s.partner())
        post.sent(box.at[1], hsem.at[1], s.sibling())
        post.arrived(hid.at[:, s.c], hsem.at[2], s.across())
        post.arrived(hid.at[:, 1 - s.c], hsem.at[3], s.partner())

    post.sent(wa.at[0:7, :, early], zsem.at[1], s.at_z(1)[1])
    post.sent(wa.at[0:7, :, late], zsem.at[5], s.at_z(1)[1])
    post.sent(wb.at[0:7], zsem.at[3], s.at_z(1)[1])
    post.sent(small, misc.at[6], s.sibling())
    post.sent(kv.at[:, s.c], misc.at[7], s.sibling())
    post.sent(part.at[0:7], rr.at[32], s.at_z(1)[1])
    for each in (plane_a, plane_o, plane_b, ring1, ring2):
        each.finish()


def tokw_ready(s, trade, tok, tokw, lsem, half):
    if half == 2:

        @pl.when(s.same)
        def _():
            pltpu.make_async_copy(tok, tokw, lsem.at[2]).wait()

        @pl.when(jnp.logical_not(s.same))
        def _():
            trade(tok, tokw, 2).wait_recv()

    return tokw


def layer(*args):
    dma = lambda *n: pltpu.SemaphoreType.DMA(n)
    return pl.pallas_call(
        layer_kernel,
        out_shape=(jax.ShapeDtypeStruct((ROWS, D), BF16), jax.ShapeDtypeStruct((8, 2, ROWS, 256), BF16)),
        in_specs=[ANY] * 8 + [VM] * 3 + [SM] + [VM] * 3,
        out_specs=(ANY, ANY),
        scratch_shapes=[
            pltpu.VMEM((ROWS, D), BF16),
            *[pltpu.VMEM((8, n), F32) for n in (2048, 2048, 4096, 4096, 4096, 4096, 4096)],
            pltpu.VMEM((8, 8, CA), BF16),
            pltpu.VMEM((8, 8, CB), BF16),
            pltpu.VMEM((ROWS, D), BF16),
            pltpu.VMEM((8, SPAN), F32),
            pltpu.VMEM((8, SPAN), F32),
            pltpu.VMEM((ROWS, D), BF16),
            pltpu.VMEM((4, 2, 2, 8, 2, 8, CA), BF16),
            pltpu.VMEM((4, 2, 2, 8, 2, 8, CB), BF16),
            pltpu.VMEM((8, ROWS, D), BF16),
            pltpu.VMEM((8, ROWS, D), BF16),
            pltpu.VMEM((8, 2, ROWS, 768), BF16),
            pltpu.VMEM((8, ROWS, DK), F32),
            pltpu.VMEM((8, ROWS, DK), F32),
            pltpu.VMEM((512, DK), BF16),
            pltpu.VMEM((512, DV), BF16),
            pltpu.VMEM((8, SPAN), F32),
            pltpu.VMEM((SPAN, 128), F32),
            pltpu.VMEM((512, DV), BF16),
            pltpu.VMEM((8, ROWS, D), BF16),
            pltpu.VMEM((2, 4, ROWS, D), BF16),
            pltpu.VMEM((2, 3, ROWS, D), BF16),
            pltpu.VMEM((ROWS, D), BF16),
            pltpu.VMEM((2, 8, ROWS, 256), BF16),
            dma(6), dma(17), dma(33), dma(33),
            dma(6, PlaneGather.FIRST), dma(6, PlaneGather.SECOND), dma(6, PlaneGather.ENDS),
            dma(8), dma(5), dma(5), dma(8),
        ],
        compiler_params=pltpu.CompilerParams(collective_id=0, has_side_effects=True, vmem_limit_bytes=VMEM_LIMIT),
        name="layer",
    )(*args)


def finish_kernel(res, hid, res_out, hid_out, res_box, hid_box, into, outof):
    quarters = [pl.ds(256 * n, 256) for n in range(4)]
    steps = [(res, res_box, res_out)] + [(hid.at[r], hid_box.at[r], hid_out.at[r]) for r in quarters]
    loads = [local(src, box, into.at[n]) for n, (src, box, _) in enumerate(steps)]
    stores = []
    for n, (_, box, dst) in enumerate(steps):
        loads[n].wait()
        stores.append(local(box, dst, outof.at[n]))
    for store in stores:
        store.wait()


def finish(res, hid):
    return pl.pallas_call(
        finish_kernel,
        out_shape=(jax.ShapeDtypeStruct(res.shape, BF16), jax.ShapeDtypeStruct(hid.shape, BF16)),
        in_specs=[ANY] * 2,
        out_specs=(ANY, ANY),
        scratch_shapes=[
            pltpu.VMEM(res.shape, BF16),
            pltpu.VMEM(hid.shape, BF16),
            pltpu.SemaphoreType.DMA((5,)),
            pltpu.SemaphoreType.DMA((5,)),
        ],
        name="finish",
    )(res, hid)


def per_device(tokens, norm_gain, mlp_gain, lengths, log_decay, q, k, v, g, o, fg, fu):
    far, near, sign = turn_tables()
    res, hid = layer(
        tokens, q, k, v, g, o.T, fg, fu,
        norm_gain.reshape(1, D), mlp_gain.reshape(1, D), log_decay.T, lengths.astype(F32).reshape(1, 1), far, near, sign,
    )
    return finish(res, hid.reshape(SPAN, 256))


def solution(mesh):
    rows = P(("dp", "mp"), None)
    placed = (rows, P(), P(), P("dp"), P("dp", None), rows, rows, rows, rows, P(None, ("dp", "mp")), rows, rows)
    return jax.shard_map(
        per_device, mesh=mesh, in_specs=placed, out_specs=(rows, P("dp", "mp")), check_vma=False
    )
```
